512 devices in a mesh: tile: 64 (over z, y), scan: 8 (over x, core).
Axes of the slice: x: 4, y: 8, z: 8, core: 2. Of those that a mesh axis runs over, the one named last changes fastest.
Arguments:
- object_real: float32 [3, 64, 128, 128], P(None, 'tile'), may hold values from 0.5 to 1.5
- object_imag: float32 [3, 64, 128, 128], P(None, 'tile'), may hold values from -1 to 1
- probe_modes: float32 [2, 2, 128, 128], replicated, may hold values from -6 to 6
- measured: float32 [64, 8, 1, 128, 128], P('tile', 'scan'), may hold values from 1 to 6
- offsets: int32 [64, 8, 1, 2], P('tile', 'scan'), may hold values from 0 to 127
- live: int32 [64, 8, 1], P('tile', 'scan'), may hold values 0 or 1
Outputs:
- object_real_out: float32 [3, 64, 128, 128], P(None, 'tile')
- object_imag_out: float32 [3, 64, 128, 128], P(None, 'tile')
- probe_out: float32 [2, 2, 128, 128], replicated
The draws below stay inside these ranges and needn't reach their ends.
All inputs are finite; a program needn't handle non-finite values. No bound on the sum of `live` on one device may be relied on, other than what follows from the above.
Results may differ from the reference program's by a relative error of at most 0.0003.
Values sent between devices are 32-bit elements; how exact they have to be, the bound alone decides.
No kernel may reach another device: no remote copies, remote signals or barrier semaphores. Data moves between devices by JAX's collectives and lax.ppermute only.
A program may use at most 64 MiB of HBM per device.

```python
import math
import jax
import jax.numpy as jnp
from jax import lax

PAT = 128
MODES = 2
SLICES = 3
OB = 128
GRID = 8
ITERS = 2
SLOTS = 1
TILES = 64
GROUPS = 8
N_TILE = 64
N_SCAN = 8


def touch_ends(array, rng, least, largest):
    extent = array.shape
    place = [jax.random.randint(jax.random.fold_in(rng, axis), (), 0, extent[axis]) for axis in range(len(extent))]
    array = array.at[tuple(place)].set(least)
    longest = extent.index(max(extent))
    place[longest] = (place[longest] + 1) % extent[longest]
    return array.at[tuple(place)].set(largest)


def levels(key, extent, split, smallest, high):
    level, own = 1.0, jax.random.fold_in(key, 6)
    for axis_at, shards_of in split:
        heights = jnp.exp(jax.random.uniform(jax.random.fold_in(own, axis_at), (shards_of,), jnp.float32, smallest / len(split), high / len(split)))
        level = level * jnp.repeat(heights, extent[axis_at] // shards_of).reshape([-1 if axis == axis_at else 1 for axis in range(len(extent))])
    return level


def centred(own_key, dims, deviation, reach, cuts=(), held_as=jnp.bfloat16):
    entries = deviation * jax.random.normal(own_key, dims, jnp.float32)
    if cuts:
        entries = entries * levels(own_key, dims, cuts, -0.22, 0.18)
    return jnp.clip(entries, -reach, reach).astype(held_as)


def setup_inputs(seed: int = 0) -> dict:
    keys = jax.random.split(jax.random.key(seed), 7)
    return {
        "object_real": jnp.clip(1.0 + 0.1 * jax.random.normal(keys[0], (SLICES, TILES, OB, OB), jnp.float32), 0.5, 1.5),
        "object_imag": centred(keys[1], (SLICES, TILES, OB, OB), 0.2, 1.0, ((1, 64),), jnp.float32),
        "probe_modes": centred(keys[2], (MODES, 2, PAT, PAT), 1.0, 6.0, (), jnp.float32),
        "measured": jnp.clip(1.0 + 5.0 * jax.random.uniform(keys[3], (TILES, GROUPS, SLOTS, PAT, PAT), jnp.float32) ** levels(keys[3], (TILES, GROUPS, SLOTS, PAT, PAT), ((0, 64), (1, 8)), -0.2, 0.2), 1.0, 6.0),
        "offsets": touch_ends(jax.random.randint(keys[4], (TILES, GROUPS, SLOTS, 2), 0, OB), jax.random.fold_in(keys[4], 1), 0, OB - 1).astype(jnp.int32),
        "live": touch_ends((jax.random.randint(keys[5], (TILES, GROUPS, SLOTS), 0, 4) < 3).astype(jnp.int32), jax.random.fold_in(keys[5], 1), 0, 1),
    }


object_rate = 0.008
probe_rate = 0.03

def kernel_parts():
    positions = jnp.arange(PAT, dtype=jnp.int32)
    frequency = jnp.where(positions < PAT // 2, positions, positions - PAT).astype(jnp.float32)
    phases = -4.0 * math.pi * (frequency[:, None] ** 2 + frequency[None, :] ** 2) / (PAT * PAT)
    return lax.complex(jnp.cos(phases), jnp.sin(phases))

def slot_loss(patch_cells, mode_values, target, weight, kernel):
    layers = lax.complex(patch_cells[0], patch_cells[1])
    wave_field = lax.complex(mode_values[:, 0], mode_values[:, 1])
    for depth_index in range(SLICES):
        wave_field = wave_field * layers[depth_index]
        if depth_index < SLICES - 1:
            wave_field = jnp.fft.ifft2(kernel * jnp.fft.fft2(wave_field, norm='ortho'), norm='ortho')
    far_field = jnp.fft.fft2(wave_field, norm='ortho')
    intensity = lax.optimization_barrier(jnp.sum(jnp.real(far_field) ** 2 + jnp.imag(far_field) ** 2, axis=0))
    return 0.5 * weight * jnp.sum((intensity - target) ** 2)

def reference(object_real, object_imag, probe_modes, measured, offsets, live):
    kernel = kernel_parts()
    obj_state = jnp.stack([object_real, object_imag])
    targets = measured.reshape(-1, PAT, PAT)
    shifts = offsets.reshape(-1, 2).astype(jnp.int32)
    weights = live.reshape(-1).astype(jnp.float32)
    owners = (jnp.arange(N_TILE * N_SCAN * SLOTS, dtype=jnp.int32) // (N_SCAN * SLOTS)).astype(jnp.int32)
    anchor = jnp.zeros((), jnp.int32)
    for iteration in range(ITERS):
        current_state = obj_state
        current_probe = probe_modes

        def visit_slot(running, inputs):
            grad_tiles, grad_probe = running
            owner_tile, shift_pair, target, weight = inputs
            members = jnp.stack([owner_tile, owner_tile + 1, owner_tile + GRID, owner_tile + GRID + 1]).astype(jnp.int32) % N_TILE
            pieces = jnp.take(current_state, members, axis=2)
            upper_half = jnp.concatenate([pieces[:, :, 0], pieces[:, :, 1]], axis=-1)
            lower_half = jnp.concatenate([pieces[:, :, 2], pieces[:, :, 3]], axis=-1)
            window = jnp.concatenate([upper_half, lower_half], axis=-2)
            starts = (anchor, anchor, shift_pair[0].astype(jnp.int32), shift_pair[1].astype(jnp.int32))
            patch_cells = lax.dynamic_slice(window, starts, (2, SLICES, PAT, PAT))
            _, pullback = jax.vjp(lambda cell_values, mode_values: slot_loss(cell_values, mode_values, target, weight, kernel), patch_cells, current_probe)
            grad_patch, grad_modes = pullback(jnp.ones((), jnp.float32))
            grad_window = lax.dynamic_update_slice(jnp.zeros_like(window), grad_patch, starts)
            quarters = jnp.stack([grad_window[:, :, :OB, :OB], grad_window[:, :, :OB, OB:], grad_window[:, :, OB:, :OB], grad_window[:, :, OB:, OB:]], axis=2)
            grad_tiles = grad_tiles.at[:, :, members].add(quarters)
            return ((grad_tiles, grad_probe + grad_modes), None)
        initial = (jnp.zeros_like(obj_state), jnp.zeros_like(probe_modes))
        (grad_tiles, grad_probe), _ = lax.scan(visit_slot, initial, (owners, shifts, targets, weights))
        obj_state = obj_state - object_rate / (SLOTS * N_SCAN) * grad_tiles
        probe_modes = probe_modes - probe_rate / (SLOTS * N_TILE * N_SCAN) * grad_probe
    return (obj_state[0], obj_state[1], probe_modes)
```

```python
import math

import jax
import jax.numpy as jnp
from jax import lax
from jax.sharding import PartitionSpec as P

GRID = 8
ITERS = 2


object_rate = 0.008
probe_rate = 0.03


def shifted(shard, axis, by):
    size = lax.axis_size(axis)
    return lax.ppermute(shard, axis, [(i, (i + by) % size) for i in range(size)])


def make_tables(pattern_side):
    positions = lax.iota(jnp.int32, pattern_side)
    product = positions[:, None] * positions[None, :] % pattern_side
    angles = 2.0 * math.pi / pattern_side * product.astype(jnp.float32)
    scaling = 1.0 / math.sqrt(pattern_side)
    frequency = jnp.where(
        positions < pattern_side // 2, positions, positions - pattern_side
    ).astype(jnp.float32)
    phases = (
        -4.0
        * math.pi
        * (frequency[:, None] ** 2 + frequency[None, :] ** 2)
        / (pattern_side * pattern_side)
    )
    return (jnp.cos(angles) * scaling, jnp.sin(angles) * scaling, jnp.cos(phases), jnp.sin(phases))


def from_left(matrix, values):
    return jnp.einsum("jk,mkl->mjl", matrix, values, precision=lax.Precision.HIGHEST)


def from_right(values, matrix):
    return jnp.einsum("mjk,kl->mjl", values, matrix, precision=lax.Precision.HIGHEST)


def transform(part_real, part_imag, tables, sign):
    cosine, sine_table = (tables[0], tables[1])
    left_real = from_left(cosine, part_real) + sign * from_left(sine_table, part_imag)
    left_imag = from_left(cosine, part_imag) - sign * from_left(sine_table, part_real)
    out_real = from_right(left_real, cosine) + sign * from_right(left_imag, sine_table)
    out_imag = from_right(left_imag, cosine) - sign * from_right(left_real, sine_table)
    return (out_real, out_imag)


def slot_loss(patch_cells, mode_values, target, weight, tables):
    depth_count = patch_cells.shape[1]
    wave_real, wave_imag = (mode_values[:, 0], mode_values[:, 1])
    for depth_index in range(depth_count):
        cell_real = patch_cells[0, depth_index]
        cell_imag = patch_cells[1, depth_index]
        wave_real, wave_imag = (
            wave_real * cell_real - wave_imag * cell_imag,
            wave_real * cell_imag + wave_imag * cell_real,
        )
        if depth_index < depth_count - 1:
            freq_real, freq_imag = transform(wave_real, wave_imag, tables, 1.0)
            kern_real, kern_imag = (tables[2], tables[3])
            freq_real, freq_imag = (
                freq_real * kern_real - freq_imag * kern_imag,
                freq_real * kern_imag + freq_imag * kern_real,
            )
            wave_real, wave_imag = transform(freq_real, freq_imag, tables, -1.0)
    far_real, far_imag = transform(wave_real, wave_imag, tables, 1.0)
    intensity = jnp.sum(far_real**2 + far_imag**2, axis=0)
    return 0.5 * weight * jnp.sum((intensity - target) ** 2)


def xor_sum(values, axis):
    size = lax.axis_size(axis)
    step = 1
    while step < size:
        values = values + lax.ppermute(values, axis, [(i, i ^ step) for i in range(size)])
        step *= 2
    return values


def local(object_real, object_imag, probe_modes, measured, offsets, live):
    slices = object_real.shape[0]
    block_side = object_real.shape[2]
    pattern_side = probe_modes.shape[2]
    slot_count = measured.shape[2]
    tile_count = lax.axis_size("tile")
    group_count = lax.axis_size("scan")
    tables = make_tables(pattern_side)
    anchor = jnp.zeros((), jnp.int32)
    obj_state = jnp.stack([object_real[:, 0], object_imag[:, 0]])
    parts = 2 * slices
    modes = probe_modes.shape[0]
    pending = None
    for iteration in range(ITERS + 1):
        if pending is not None:
            probe_sum = pending
            for step in (2, 4, 2 * GRID, 4 * GRID):
                probe_sum = probe_sum + shifted(probe_sum, "tile", step)
            probe_modes = (
                probe_modes - probe_rate / (slot_count * tile_count * group_count) * probe_sum
            )
        if iteration == ITERS:
            break
        right_part = shifted(obj_state, "tile", -1)
        upper_half = jnp.concatenate([obj_state, right_part], axis=-1)
        lower_half = shifted(upper_half, "tile", -GRID)
        canvas = jnp.concatenate([upper_half, lower_half], axis=-2)
        current_probe = probe_modes

        grad_canvas = jnp.zeros_like(canvas)
        grad_probe = jnp.zeros_like(probe_modes)
        for slot_index in range(slot_count):
            row_start = offsets[0, 0, slot_index, 0]
            col_start = offsets[0, 0, slot_index, 1]
            starts = (anchor, anchor, row_start, col_start)
            patch_cells = lax.dynamic_slice(canvas, starts, (2, slices, pattern_side, pattern_side))
            target = measured[0, 0, slot_index]
            weight = live[0, 0, slot_index].astype(jnp.float32)
            _, pullback = jax.vjp(
                lambda cell_values, mode_values: slot_loss(
                    cell_values, mode_values, target, weight, tables
                ),
                patch_cells,
                current_probe,
            )
            grad_patch, grad_modes = pullback(jnp.ones((), jnp.float32))
            current = lax.dynamic_slice(
                grad_canvas, starts, (2, slices, pattern_side, pattern_side)
            )
            grad_canvas = lax.dynamic_update_slice(grad_canvas, current + grad_patch, starts)
            grad_probe = grad_probe + grad_modes
        planes = lambda a: a.reshape(-1, block_side, block_side)
        probe_planes = planes(grad_probe)
        sent_down = jnp.concatenate(
            [
                planes(grad_canvas[:, :, block_side:, :block_side]),
                planes(grad_canvas[:, :, block_side:, block_side:]),
                probe_planes,
            ]
        )
        came_down = shifted(sent_down, "tile", GRID)
        own_part = planes(grad_canvas[:, :, :block_side, :block_side]) + came_down[:parts]
        right_side = planes(grad_canvas[:, :, :block_side, block_side:]) + came_down[parts : 2 * parts]
        probe_partial = probe_planes + came_down[2 * parts :]
        sent_left = jnp.concatenate([right_side, probe_partial])
        came_left = shifted(sent_left, "tile", 1)
        own_part = own_part + came_left[:parts]
        probe_partial = probe_partial + came_left[parts:]
        reduced = xor_sum(jnp.concatenate([own_part, probe_partial]), "scan")
        grad_total = reduced[:parts].reshape(obj_state.shape)
        pending = reduced[parts:].reshape(probe_modes.shape)
        obj_state = obj_state - object_rate / (slot_count * group_count) * grad_total
    return (obj_state[0][:, None], obj_state[1][:, None], probe_modes)


def solution(mesh):
    placed = (
        P(None, "tile", None, None),
        P(None, "tile", None, None),
        P(),
        P("tile", "scan", None, None, None),
        P("tile", "scan", None, None),
        P("tile", "scan", None),
    )
    return jax.shard_map(
        local,
        mesh=mesh,
        in_specs=placed,
        out_specs=(P(None, "tile", None, None), P(None, "tile", None, None), P()),
        check_vma=False,
    )
```

```python
import math

import jax
import jax.numpy as jnp
from jax import lax
from jax.experimental import pallas as pl
from jax.experimental.pallas import tpu as pltpu
from jax.sharding import PartitionSpec as P

GRID = 8
ITERS = 2


object_rate = 0.008
probe_rate = 0.03


def shifted(shard, axis, by):
    size = lax.axis_size(axis)
    return lax.ppermute(shard, axis, [(i, (i + by) % size) for i in range(size)])


def make_tables(pattern_side):
    positions = lax.iota(jnp.int32, pattern_side)
    product = positions[:, None] * positions[None, :] % pattern_side
    angles = 2.0 * math.pi / pattern_side * product.astype(jnp.float32)
    scaling = 1.0 / math.sqrt(pattern_side)
    frequency = jnp.where(
        positions < pattern_side // 2, positions, positions - pattern_side
    ).astype(jnp.float32)
    phases = (
        -4.0
        * math.pi
        * (frequency[:, None] ** 2 + frequency[None, :] ** 2)
        / (pattern_side * pattern_side)
    )
    return (jnp.cos(angles) * scaling, jnp.sin(angles) * scaling, jnp.cos(phases), jnp.sin(phases))


def from_left(matrix, values):
    return jnp.einsum("jk,mkl->mjl", matrix, values, precision=lax.Precision.HIGHEST)


def from_right(values, matrix):
    return jnp.einsum("mjk,kl->mjl", values, matrix, precision=lax.Precision.HIGHEST)


def transform(part_real, part_imag, tables, sign):
    cosine, sine_table = (tables[0], tables[1])
    left_real = from_left(cosine, part_real) + sign * from_left(sine_table, part_imag)
    left_imag = from_left(cosine, part_imag) - sign * from_left(sine_table, part_real)
    out_real = from_right(left_real, cosine) + sign * from_right(left_imag, sine_table)
    out_imag = from_right(left_imag, cosine) - sign * from_right(left_real, sine_table)
    return (out_real, out_imag)


def slot_loss(patch_cells, mode_values, target, weight, tables):
    depth_count = patch_cells.shape[1]
    wave_real, wave_imag = (mode_values[:, 0], mode_values[:, 1])
    for depth_index in range(depth_count):
        cell_real = patch_cells[0, depth_index]
        cell_imag = patch_cells[1, depth_index]
        wave_real, wave_imag = (
            wave_real * cell_real - wave_imag * cell_imag,
            wave_real * cell_imag + wave_imag * cell_real,
        )
        if depth_index < depth_count - 1:
            freq_real, freq_imag = transform(wave_real, wave_imag, tables, 1.0)
            kern_real, kern_imag = (tables[2], tables[3])
            freq_real, freq_imag = (
                freq_real * kern_real - freq_imag * kern_imag,
                freq_real * kern_imag + freq_imag * kern_real,
            )
            wave_real, wave_imag = transform(freq_real, freq_imag, tables, -1.0)
    far_real, far_imag = transform(wave_real, wave_imag, tables, 1.0)
    intensity = jnp.sum(far_real**2 + far_imag**2, axis=0)
    return 0.5 * weight * jnp.sum((intensity - target) ** 2)


def slot_kernel(cells_ref, probe_ref, target_ref, weight_ref, tab_ref, gcells_ref, gprobe_ref):
    cosine, sine_table, kern_real, kern_imag = (tab_ref[0], tab_ref[1], tab_ref[2], tab_ref[3])

    def dot(a, b):
        return jnp.dot(a, b, precision=lax.Precision.HIGHEST, preferred_element_type=jnp.float32)

    def forward(xr, xi):
        lr = dot(cosine, xr) + dot(sine_table, xi)
        li = dot(cosine, xi) - dot(sine_table, xr)
        return (dot(lr, cosine) + dot(li, sine_table), dot(li, cosine) - dot(lr, sine_table))

    def inverse(xr, xi):
        lr = dot(cosine, xr) - dot(sine_table, xi)
        li = dot(cosine, xi) + dot(sine_table, xr)
        return (dot(lr, cosine) - dot(li, sine_table), dot(li, cosine) + dot(lr, sine_table))

    def mul(a, b):
        return (a[0] * b[0] - a[1] * b[1], a[0] * b[1] + a[1] * b[0])

    def mul_conj(a, b):
        return (a[0] * b[0] + a[1] * b[1], a[1] * b[0] - a[0] * b[1])

    kern = (kern_real, kern_imag)
    propagate = lambda x: inverse(*mul(forward(*x), kern))
    propagate_adjoint = lambda x: inverse(*mul_conj(forward(*x), kern))
    depth_count = cells_ref.shape[1]
    mode_count = probe_ref.shape[0]
    layers = [(cells_ref[0, d], cells_ref[1, d]) for d in range(depth_count)]
    saved = []
    intensity = None
    for m in range(mode_count):
        wave = (probe_ref[m, 0], probe_ref[m, 1])
        inputs = []
        for d in range(depth_count):
            inputs.append(wave)
            wave = mul(wave, layers[d])
            if d < depth_count - 1:
                wave = propagate(wave)
        far = forward(*wave)
        saved.append((inputs, far))
        power = far[0] * far[0] + far[1] * far[1]
        intensity = power if intensity is None else intensity + power
    residual = weight_ref[...] * (intensity - target_ref[...])
    layer_grads = [None] * depth_count
    for m in range(mode_count):
        inputs, far = saved[m]
        grad = inverse(2.0 * residual * far[0], 2.0 * residual * far[1])
        for d in reversed(range(depth_count)):
            term = mul_conj(grad, inputs[d])
            if layer_grads[d] is None:
                layer_grads[d] = term
            else:
                layer_grads[d] = (layer_grads[d][0] + term[0], layer_grads[d][1] + term[1])
            grad = mul_conj(grad, layers[d])
            if d > 0:
                grad = propagate_adjoint(grad)
        gprobe_ref[m, 0] = grad[0]
        gprobe_ref[m, 1] = grad[1]
    for d in range(depth_count):
        gcells_ref[0, d] = layer_grads[d][0]
        gcells_ref[1, d] = layer_grads[d][1]


def slot_grad(patch_cells, mode_values, target, weight, tables):
    tab = jnp.stack(tables)
    side = target.shape[-1]
    dots = 2 * mode_values.shape[0] * 10 * 8
    return pl.pallas_call(
        slot_kernel,
        out_shape=(
            jax.ShapeDtypeStruct(patch_cells.shape, jnp.float32),
            jax.ShapeDtypeStruct(mode_values.shape, jnp.float32),
        ),
        in_specs=[pl.BlockSpec(memory_space=pltpu.VMEM)] * 5,
        out_specs=(pl.BlockSpec(memory_space=pltpu.VMEM), pl.BlockSpec(memory_space=pltpu.VMEM)),
        cost_estimate=pl.CostEstimate(
            flops=dots * 2 * side**3, bytes_accessed=4 * side * side * 22, transcendentals=0
        ),
    )(patch_cells, mode_values, target, weight.reshape(1, 1), tab)


def xor_sum(values, axis):
    size = lax.axis_size(axis)
    step = 1
    while step < size:
        values = values + lax.ppermute(values, axis, [(i, i ^ step) for i in range(size)])
        step *= 2
    return values


def local(object_real, object_imag, probe_modes, measured, offsets, live):
    slices = object_real.shape[0]
    block_side = object_real.shape[2]
    pattern_side = probe_modes.shape[2]
    slot_count = measured.shape[2]
    tile_count = lax.axis_size("tile")
    group_count = lax.axis_size("scan")
    tables = make_tables(pattern_side)
    anchor = jnp.zeros((), jnp.int32)
    obj_state = jnp.stack([object_real[:, 0], object_imag[:, 0]])
    parts = 2 * slices
    modes = probe_modes.shape[0]
    pending = None
    for iteration in range(ITERS + 1):
        if pending is not None:
            probe_sum = pending
            for step in (2, 4, 2 * GRID, 4 * GRID):
                probe_sum = probe_sum + shifted(probe_sum, "tile", step)
            probe_modes = (
                probe_modes - probe_rate / (slot_count * tile_count * group_count) * probe_sum
            )
        if iteration == ITERS:
            break
        right_part = shifted(obj_state, "tile", -1)
        upper_half = jnp.concatenate([obj_state, right_part], axis=-1)
        lower_half = shifted(upper_half, "tile", -GRID)
        canvas = jnp.concatenate([upper_half, lower_half], axis=-2)
        current_probe = probe_modes

        grad_canvas = jnp.zeros_like(canvas)
        grad_probe = jnp.zeros_like(probe_modes)
        for slot_index in range(slot_count):
            row_start = offsets[0, 0, slot_index, 0]
            col_start = offsets[0, 0, slot_index, 1]
            starts = (anchor, anchor, row_start, col_start)
            patch_cells = lax.dynamic_slice(canvas, starts, (2, slices, pattern_side, pattern_side))
            target = measured[0, 0, slot_index]
            weight = live[0, 0, slot_index].astype(jnp.float32)
            grad_patch, grad_modes = slot_grad(patch_cells, current_probe, target, weight, tables)
            current = lax.dynamic_slice(
                grad_canvas, starts, (2, slices, pattern_side, pattern_side)
            )
            grad_canvas = lax.dynamic_update_slice(grad_canvas, current + grad_patch, starts)
            grad_probe = grad_probe + grad_modes
        planes = lambda a: a.reshape(-1, block_side, block_side)
        probe_planes = planes(grad_probe)
        sent_down = jnp.concatenate(
            [
                planes(grad_canvas[:, :, block_side:, :block_side]),
                planes(grad_canvas[:, :, block_side:, block_side:]),
                probe_planes,
            ]
        )
        came_down = shifted(sent_down, "tile", GRID)
        own_part = planes(grad_canvas[:, :, :block_side, :block_side]) + came_down[:parts]
        right_side = planes(grad_canvas[:, :, :block_side, block_side:]) + came_down[parts : 2 * parts]
        probe_partial = probe_planes + came_down[2 * parts :]
        sent_left = jnp.concatenate([right_side, probe_partial])
        came_left = shifted(sent_left, "tile", 1)
        own_part = own_part + came_left[:parts]
        probe_partial = probe_partial + came_left[parts:]
        reduced = xor_sum(jnp.concatenate([own_part, probe_partial]), "scan")
        grad_total = reduced[:parts].reshape(obj_state.shape)
        pending = reduced[parts:].reshape(probe_modes.shape)
        obj_state = obj_state - object_rate / (slot_count * group_count) * grad_total
    return (obj_state[0][:, None], obj_state[1][:, None], probe_modes)


def solution(mesh):
    placed = (
        P(None, "tile", None, None),
        P(None, "tile", None, None),
        P(),
        P("tile", "scan", None, None, None),
        P("tile", "scan", None, None),
        P("tile", "scan", None),
    )
    return jax.shard_map(
        local,
        mesh=mesh,
        in_specs=placed,
        out_specs=(P(None, "tile", None, None), P(None, "tile", None, None), P()),
        check_vma=False,
    )
```

```python
import math

import jax
import jax.numpy as jnp
from jax import lax
from jax.experimental import pallas as pl
from jax.experimental.pallas import tpu as pltpu
from jax.sharding import PartitionSpec as P

GRID = 8
ITERS = 2


object_rate = 0.008
probe_rate = 0.03


def shifted(shard, axis, by):
    size = lax.axis_size(axis)
    return lax.ppermute(shard, axis, [(i, (i + by) % size) for i in range(size)])


def make_tables(pattern_side):
    positions = lax.iota(jnp.int32, pattern_side)
    product = positions[:, None] * positions[None, :] % pattern_side
    angles = 2.0 * math.pi / pattern_side * product.astype(jnp.float32)
    scaling = 1.0 / math.sqrt(pattern_side)
    frequency = jnp.where(
        positions < pattern_side // 2, positions, positions - pattern_side
    ).astype(jnp.float32)
    phases = (
        -4.0
        * math.pi
        * (frequency[:, None] ** 2 + frequency[None, :] ** 2)
        / (pattern_side * pattern_side)
    )
    return (jnp.cos(angles) * scaling, jnp.sin(angles) * scaling, jnp.cos(phases), jnp.sin(phases))


def from_left(matrix, values):
    return jnp.einsum("jk,mkl->mjl", matrix, values, precision=lax.Precision.HIGHEST)


def from_right(values, matrix):
    return jnp.einsum("mjk,kl->mjl", values, matrix, precision=lax.Precision.HIGHEST)


def transform(part_real, part_imag, tables, sign):
    cosine, sine_table = (tables[0], tables[1])
    left_real = from_left(cosine, part_real) + sign * from_left(sine_table, part_imag)
    left_imag = from_left(cosine, part_imag) - sign * from_left(sine_table, part_real)
    out_real = from_right(left_real, cosine) + sign * from_right(left_imag, sine_table)
    out_imag = from_right(left_imag, cosine) - sign * from_right(left_real, sine_table)
    return (out_real, out_imag)


def slot_loss(patch_cells, mode_values, target, weight, tables):
    depth_count = patch_cells.shape[1]
    wave_real, wave_imag = (mode_values[:, 0], mode_values[:, 1])
    for depth_index in range(depth_count):
        cell_real = patch_cells[0, depth_index]
        cell_imag = patch_cells[1, depth_index]
        wave_real, wave_imag = (
            wave_real * cell_real - wave_imag * cell_imag,
            wave_real * cell_imag + wave_imag * cell_real,
        )
        if depth_index < depth_count - 1:
            freq_real, freq_imag = transform(wave_real, wave_imag, tables, 1.0)
            kern_real, kern_imag = (tables[2], tables[3])
            freq_real, freq_imag = (
                freq_real * kern_real - freq_imag * kern_imag,
                freq_real * kern_imag + freq_imag * kern_real,
            )
            wave_real, wave_imag = transform(freq_real, freq_imag, tables, -1.0)
    far_real, far_imag = transform(wave_real, wave_imag, tables, 1.0)
    intensity = jnp.sum(far_real**2 + far_imag**2, axis=0)
    return 0.5 * weight * jnp.sum((intensity - target) ** 2)


def slot_kernel(cells_ref, probe_ref, target_ref, weight_ref, tab_ref, gcells_ref, gprobe_ref):
    cosine, sine_table, kern_real, kern_imag = (tab_ref[0], tab_ref[1], tab_ref[2], tab_ref[3])

    def dot(a, b):
        return jnp.dot(a, b, precision=lax.Precision.HIGHEST, preferred_element_type=jnp.float32)

    def forward(xr, xi):
        lr = dot(cosine, xr) + dot(sine_table, xi)
        li = dot(cosine, xi) - dot(sine_table, xr)
        return (dot(lr, cosine) + dot(li, sine_table), dot(li, cosine) - dot(lr, sine_table))

    def inverse(xr, xi):
        lr = dot(cosine, xr) - dot(sine_table, xi)
        li = dot(cosine, xi) + dot(sine_table, xr)
        return (dot(lr, cosine) - dot(li, sine_table), dot(li, cosine) + dot(lr, sine_table))

    def mul(a, b):
        return (a[0] * b[0] - a[1] * b[1], a[0] * b[1] + a[1] * b[0])

    def mul_conj(a, b):
        return (a[0] * b[0] + a[1] * b[1], a[1] * b[0] - a[0] * b[1])

    kern = (kern_real, kern_imag)
    propagate = lambda x: inverse(*mul(forward(*x), kern))
    propagate_adjoint = lambda x: inverse(*mul_conj(forward(*x), kern))
    depth_count = cells_ref.shape[1]
    mode_count = probe_ref.shape[0]
    layers = [(cells_ref[0, d], cells_ref[1, d]) for d in range(depth_count)]
    saved = []
    intensity = None
    for m in range(mode_count):
        wave = (probe_ref[m, 0], probe_ref[m, 1])
        inputs = []
        for d in range(depth_count):
            inputs.append(wave)
            wave = mul(wave, layers[d])
            if d < depth_count - 1:
                wave = propagate(wave)
        far = forward(*wave)
        saved.append((inputs, far))
        power = far[0] * far[0] + far[1] * far[1]
        intensity = power if intensity is None else intensity + power
    residual = weight_ref[...] * (intensity - target_ref[...])
    layer_grads = [None] * depth_count
    for m in range(mode_count):
        inputs, far = saved[m]
        grad = inverse(2.0 * residual * far[0], 2.0 * residual * far[1])
        for d in reversed(range(depth_count)):
            term = mul_conj(grad, inputs[d])
            if layer_grads[d] is None:
                layer_grads[d] = term
            else:
                layer_grads[d] = (layer_grads[d][0] + term[0], layer_grads[d][1] + term[1])
            grad = mul_conj(grad, layers[d])
            if d > 0:
                grad = propagate_adjoint(grad)
        gprobe_ref[m, 0] = grad[0]
        gprobe_ref[m, 1] = grad[1]
    for d in range(depth_count):
        gcells_ref[0, d] = layer_grads[d][0]
        gcells_ref[1, d] = layer_grads[d][1]


def slot_grad(patch_cells, mode_values, target, weight, tables):
    tab = jnp.stack(tables)
    side = target.shape[-1]
    dots = 2 * mode_values.shape[0] * 10 * 8
    return pl.pallas_call(
        slot_kernel,
        out_shape=(
            jax.ShapeDtypeStruct(patch_cells.shape, jnp.float32),
            jax.ShapeDtypeStruct(mode_values.shape, jnp.float32),
        ),
        in_specs=[pl.BlockSpec(memory_space=pltpu.VMEM)] * 5,
        out_specs=(pl.BlockSpec(memory_space=pltpu.VMEM), pl.BlockSpec(memory_space=pltpu.VMEM)),
        cost_estimate=pl.CostEstimate(
            flops=dots * 2 * side**3, bytes_accessed=4 * side * side * 22, transcendentals=0
        ),
    )(patch_cells, mode_values, target, weight.reshape(1, 1), tab)


def xor_sum(values, axis, steps=None):
    size = lax.axis_size(axis)
    if steps is None:
        steps = [1 << bit for bit in range(size.bit_length() - 1)]
    for step in steps:
        values = values + lax.ppermute(values, axis, [(i, i ^ step) for i in range(size)])
    return values


def local(object_real, object_imag, probe_modes, measured, offsets, live):
    slices = object_real.shape[0]
    block_side = object_real.shape[2]
    pattern_side = probe_modes.shape[2]
    slot_count = measured.shape[2]
    tile_count = lax.axis_size("tile")
    group_count = lax.axis_size("scan")
    tables = make_tables(pattern_side)
    anchor = jnp.zeros((), jnp.int32)
    obj_state = jnp.stack([object_real[:, 0], object_imag[:, 0]])
    parts = 2 * slices
    tile_bits = [1 << bit for bit in range(tile_count.bit_length() - 1)]
    first_bits = [b for b in tile_bits if b < GRID]
    second_bits = [b for b in tile_bits if b >= GRID]
    pending = None
    for iteration in range(ITERS + 1):
        if iteration == ITERS:
            probe_sum = xor_sum(pending, "tile", second_bits)
            probe_modes = (
                probe_modes - probe_rate / (slot_count * tile_count * group_count) * probe_sum
            )
            break
        probe_sum = pending
        if pending is not None:
            probe_sum = xor_sum(probe_sum, "tile", second_bits[:1])
        right_part = shifted(obj_state, "tile", -1)
        upper_half = jnp.concatenate([obj_state, right_part], axis=-1)
        if pending is not None:
            upper_half, probe_sum = lax.optimization_barrier((upper_half, probe_sum))
            probe_sum = xor_sum(probe_sum, "tile", second_bits[1:])
            probe_modes = (
                probe_modes - probe_rate / (slot_count * tile_count * group_count) * probe_sum
            )
        lower_half = shifted(upper_half, "tile", -GRID)
        canvas = jnp.concatenate([upper_half, lower_half], axis=-2)
        current_probe = probe_modes

        grad_canvas = jnp.zeros_like(canvas)
        grad_probe = jnp.zeros_like(probe_modes)
        for slot_index in range(slot_count):
            row_start = offsets[0, 0, slot_index, 0]
            col_start = offsets[0, 0, slot_index, 1]
            starts = (anchor, anchor, row_start, col_start)
            patch_cells = lax.dynamic_slice(canvas, starts, (2, slices, pattern_side, pattern_side))
            target = measured[0, 0, slot_index]
            weight = live[0, 0, slot_index].astype(jnp.float32)
            grad_patch, grad_modes = slot_grad(patch_cells, current_probe, target, weight, tables)
            current = lax.dynamic_slice(
                grad_canvas, starts, (2, slices, pattern_side, pattern_side)
            )
            grad_canvas = lax.dynamic_update_slice(grad_canvas, current + grad_patch, starts)
            grad_probe = grad_probe + grad_modes
        planes = lambda a: a.reshape(-1, block_side, block_side)
        sent_down = jnp.concatenate(
            [
                planes(grad_canvas[:, :, block_side:, :block_side]),
                planes(grad_canvas[:, :, block_side:, block_side:]),
            ]
        )
        pair = lambda a, b: lax.optimization_barrier((a, b))
        probe_partial = xor_sum(grad_probe, "scan", [1])
        sent_down, probe_partial = pair(sent_down, probe_partial)
        came_down = shifted(sent_down, "tile", GRID)
        probe_partial = xor_sum(probe_partial, "scan", [2])
        own_part = planes(grad_canvas[:, :, :block_side, :block_side]) + came_down[:parts]
        right_side = planes(grad_canvas[:, :, :block_side, block_side:]) + came_down[parts:]
        right_side, probe_partial = pair(right_side, probe_partial)
        came_left = shifted(right_side, "tile", 1)
        probe_partial = xor_sum(probe_partial, "scan", [4])
        own_part = own_part + came_left
        for step in (1, 2, 4):
            own_part, probe_partial = pair(own_part, probe_partial)
            own_part = xor_sum(own_part, "scan", [step])
            probe_partial = xor_sum(probe_partial, "tile", [step])
        grad_total = own_part.reshape(obj_state.shape)
        own_part, probe_partial = pair(own_part, probe_partial)
        pending = probe_partial
        obj_state = obj_state - object_rate / (slot_count * group_count) * grad_total
    return (obj_state[0][:, None], obj_state[1][:, None], probe_modes)


def solution(mesh):
    placed = (
        P(None, "tile", None, None),
        P(None, "tile", None, None),
        P(),
        P("tile", "scan", None, None, None),
        P("tile", "scan", None, None),
        P("tile", "scan", None),
    )
    return jax.shard_map(
        local,
        mesh=mesh,
        in_specs=placed,
        out_specs=(P(None, "tile", None, None), P(None, "tile", None, None), P()),
        check_vma=False,
    )
```

```python
import math

import jax
import jax.numpy as jnp
from jax import lax
from jax.experimental import pallas as pl
from jax.experimental.pallas import tpu as pltpu
from jax.sharding import PartitionSpec as P

GRID = 8
ITERS = 2


object_rate = 0.008
probe_rate = 0.03


def shifted(shard, axis, by):
    size = lax.axis_size(axis)
    return lax.ppermute(shard, axis, [(i, (i + by) % size) for i in range(size)])


def make_tables(pattern_side):
    positions = lax.iota(jnp.int32, pattern_side)
    product = positions[:, None] * positions[None, :] % pattern_side
    angles = 2.0 * math.pi / pattern_side * product.astype(jnp.float32)
    scaling = 1.0 / math.sqrt(pattern_side)
    frequency = jnp.where(
        positions < pattern_side // 2, positions, positions - pattern_side
    ).astype(jnp.float32)
    phases = (
        -4.0
        * math.pi
        * (frequency[:, None] ** 2 + frequency[None, :] ** 2)
        / (pattern_side * pattern_side)
    )
    return (jnp.cos(angles) * scaling, jnp.sin(angles) * scaling, jnp.cos(phases), jnp.sin(phases))


def from_left(matrix, values):
    return jnp.einsum("jk,mkl->mjl", matrix, values, precision=lax.Precision.HIGHEST)


def from_right(values, matrix):
    return jnp.einsum("mjk,kl->mjl", values, matrix, precision=lax.Precision.HIGHEST)


def transform(part_real, part_imag, tables, sign):
    cosine, sine_table = (tables[0], tables[1])
    left_real = from_left(cosine, part_real) + sign * from_left(sine_table, part_imag)
    left_imag = from_left(cosine, part_imag) - sign * from_left(sine_table, part_real)
    out_real = from_right(left_real, cosine) + sign * from_right(left_imag, sine_table)
    out_imag = from_right(left_imag, cosine) - sign * from_right(left_real, sine_table)
    return (out_real, out_imag)


def slot_loss(patch_cells, mode_values, target, weight, tables):
    depth_count = patch_cells.shape[1]
    wave_real, wave_imag = (mode_values[:, 0], mode_values[:, 1])
    for depth_index in range(depth_count):
        cell_real = patch_cells[0, depth_index]
        cell_imag = patch_cells[1, depth_index]
        wave_real, wave_imag = (
            wave_real * cell_real - wave_imag * cell_imag,
            wave_real * cell_imag + wave_imag * cell_real,
        )
        if depth_index < depth_count - 1:
            freq_real, freq_imag = transform(wave_real, wave_imag, tables, 1.0)
            kern_real, kern_imag = (tables[2], tables[3])
            freq_real, freq_imag = (
                freq_real * kern_real - freq_imag * kern_imag,
                freq_real * kern_imag + freq_imag * kern_real,
            )
            wave_real, wave_imag = transform(freq_real, freq_imag, tables, -1.0)
    far_real, far_imag = transform(wave_real, wave_imag, tables, 1.0)
    intensity = jnp.sum(far_real**2 + far_imag**2, axis=0)
    return 0.5 * weight * jnp.sum((intensity - target) ** 2)


def slot_kernel(cells_ref, probe_ref, target_ref, weight_ref, tab_ref, gcells_ref, gprobe_ref):
    cosine, sine_table, kern_real, kern_imag = (tab_ref[0], tab_ref[1], tab_ref[2], tab_ref[3])

    def dot(a, b):
        return jnp.dot(a, b, precision=lax.Precision.HIGHEST, preferred_element_type=jnp.float32)

    def forward(xr, xi):
        lr = dot(cosine, xr) + dot(sine_table, xi)
        li = dot(cosine, xi) - dot(sine_table, xr)
        return (dot(lr, cosine) + dot(li, sine_table), dot(li, cosine) - dot(lr, sine_table))

    def inverse(xr, xi):
        lr = dot(cosine, xr) - dot(sine_table, xi)
        li = dot(cosine, xi) + dot(sine_table, xr)
        return (dot(lr, cosine) - dot(li, sine_table), dot(li, cosine) + dot(lr, sine_table))

    def mul(a, b):
        return (a[0] * b[0] - a[1] * b[1], a[0] * b[1] + a[1] * b[0])

    def mul_conj(a, b):
        return (a[0] * b[0] + a[1] * b[1], a[1] * b[0] - a[0] * b[1])

    kern = (kern_real, kern_imag)
    propagate = lambda x: inverse(*mul(forward(*x), kern))
    propagate_adjoint = lambda x: inverse(*mul_conj(forward(*x), kern))
    depth_count = cells_ref.shape[1]
    mode_count = probe_ref.shape[0]
    layers = [(cells_ref[0, d], cells_ref[1, d]) for d in range(depth_count)]
    saved = []
    intensity = None
    for m in range(mode_count):
        wave = (probe_ref[m, 0], probe_ref[m, 1])
        inputs = []
        for d in range(depth_count):
            inputs.append(wave)
            wave = mul(wave, layers[d])
            if d < depth_count - 1:
                wave = propagate(wave)
        far = forward(*wave)
        saved.append((inputs, far))
        power = far[0] * far[0] + far[1] * far[1]
        intensity = power if intensity is None else intensity + power
    residual = weight_ref[...] * (intensity - target_ref[...])
    layer_grads = [None] * depth_count
    for m in range(mode_count):
        inputs, far = saved[m]
        grad = inverse(2.0 * residual * far[0], 2.0 * residual * far[1])
        for d in reversed(range(depth_count)):
            term = mul_conj(grad, inputs[d])
            if layer_grads[d] is None:
                layer_grads[d] = term
            else:
                layer_grads[d] = (layer_grads[d][0] + term[0], layer_grads[d][1] + term[1])
            grad = mul_conj(grad, layers[d])
            if d > 0:
                grad = propagate_adjoint(grad)
        gprobe_ref[m, 0] = grad[0]
        gprobe_ref[m, 1] = grad[1]
    for d in range(depth_count):
        gcells_ref[0, d] = layer_grads[d][0]
        gcells_ref[1, d] = layer_grads[d][1]


def slot_grad(patch_cells, mode_values, target, weight, tables):
    tab = jnp.stack(tables)
    side = target.shape[-1]
    dots = 2 * mode_values.shape[0] * 10 * 8
    return pl.pallas_call(
        slot_kernel,
        out_shape=(
            jax.ShapeDtypeStruct(patch_cells.shape, jnp.float32),
            jax.ShapeDtypeStruct(mode_values.shape, jnp.float32),
        ),
        in_specs=[pl.BlockSpec(memory_space=pltpu.VMEM)] * 5,
        out_specs=(pl.BlockSpec(memory_space=pltpu.VMEM), pl.BlockSpec(memory_space=pltpu.VMEM)),
        cost_estimate=pl.CostEstimate(
            flops=dots * 2 * side**3, bytes_accessed=4 * side * side * 22, transcendentals=0
        ),
    )(patch_cells, mode_values, target, weight.reshape(1, 1), tab)


def xor_sum(values, axis, steps=None):
    size = lax.axis_size(axis)
    if steps is None:
        steps = [1 << bit for bit in range(size.bit_length() - 1)]
    for step in steps:
        values = values + lax.ppermute(values, axis, [(i, i ^ step) for i in range(size)])
    return values


def a2a_sum(values, axis):
    size = lax.axis_size(axis)
    flat = values.reshape(size, -1)
    part = jnp.sum(lax.all_to_all(flat, axis, 0, 0, tiled=True), axis=0, keepdims=True)
    spread = lax.all_to_all(jnp.broadcast_to(part, flat.shape), axis, 0, 0, tiled=True)
    return spread.reshape(values.shape)


def scatter_sum(values, axis):
    size = lax.axis_size(axis)
    lead, rows, cols = values.shape
    chunks = jnp.moveaxis(values.reshape(lead, size, rows // size, cols), 1, 0)
    return jnp.sum(lax.all_to_all(chunks, axis, 0, 0, tiled=True), axis=0)


def gather_rows(chunk, axis):
    size = lax.axis_size(axis)
    lead, rows, cols = chunk.shape
    spread = jnp.broadcast_to(chunk[None], (size, lead, rows, cols))
    got = lax.all_to_all(spread, axis, 0, 0, tiled=True)
    return jnp.moveaxis(got, 0, 1).reshape(lead, size * rows, cols)


def local(object_real, object_imag, probe_modes, measured, offsets, live):
    slices = object_real.shape[0]
    block_side = object_real.shape[2]
    pattern_side = probe_modes.shape[2]
    slot_count = measured.shape[2]
    tile_count = lax.axis_size("tile")
    group_count = lax.axis_size("scan")
    tables = make_tables(pattern_side)
    anchor = jnp.zeros((), jnp.int32)
    obj_state = jnp.stack([object_real[:, 0], object_imag[:, 0]])
    parts = 2 * slices
    probe_parts = probe_modes.shape[0] * probe_modes.shape[1]
    chunk_rows = block_side // group_count
    chunk_start = lax.axis_index("scan") * chunk_rows
    object_step = object_rate / (slot_count * group_count)
    probe_step = probe_rate / (slot_count * tile_count * group_count)
    planes = lambda a: a.reshape(-1, block_side, block_side)

    right_part = shifted(obj_state, "tile", -1)
    upper_half = jnp.concatenate([obj_state, right_part], axis=-1)
    lower_half = shifted(upper_half, "tile", -GRID)
    quarters = jnp.stack(
        [
            planes(obj_state),
            planes(right_part),
            planes(lower_half[..., :block_side]),
            planes(lower_half[..., block_side:]),
        ]
    )
    for iteration in range(ITERS):
        last = iteration == ITERS - 1
        canvas = jnp.concatenate(
            [
                jnp.concatenate([quarters[0], quarters[1]], axis=-1),
                jnp.concatenate([quarters[2], quarters[3]], axis=-1),
            ],
            axis=-2,
        ).reshape(2, slices, 2 * block_side, 2 * block_side)
        grad_canvas = jnp.zeros_like(canvas)
        grad_probe = jnp.zeros_like(probe_modes)
        for slot_index in range(slot_count):
            row_start = offsets[0, 0, slot_index, 0]
            col_start = offsets[0, 0, slot_index, 1]
            starts = (anchor, anchor, row_start, col_start)
            patch_cells = lax.dynamic_slice(canvas, starts, (2, slices, pattern_side, pattern_side))
            target = measured[0, 0, slot_index]
            weight = live[0, 0, slot_index].astype(jnp.float32)
            grad_patch, grad_modes = slot_grad(patch_cells, probe_modes, target, weight, tables)
            current = lax.dynamic_slice(
                grad_canvas, starts, (2, slices, pattern_side, pattern_side)
            )
            grad_canvas = lax.dynamic_update_slice(grad_canvas, current + grad_patch, starts)
            grad_probe = grad_probe + grad_modes
        grad_quarters = [
            planes(grad_canvas[:, :, :block_side, :block_side]),
            planes(grad_canvas[:, :, :block_side, block_side:]),
            planes(grad_canvas[:, :, block_side:, :block_side]),
            planes(grad_canvas[:, :, block_side:, block_side:]),
        ]
        band = scatter_sum(jnp.concatenate(grad_quarters + [planes(grad_probe)]), "scan")
        g_ul, g_ur, g_ll, g_lr = (band[q * parts : (q + 1) * parts] for q in range(4))
        probe_band = band[4 * parts :]
        flat = probe_band.reshape(tile_count, -1)
        probe_part = jnp.sum(lax.all_to_all(flat, "tile", 0, 0, tiled=True), axis=0, keepdims=True)
        probe_total = lax.all_to_all(
            jnp.broadcast_to(probe_part, flat.shape), "tile", 0, 0, tiled=True
        ).reshape(probe_band.shape)
        from_left = shifted(jnp.concatenate([g_ur, g_lr]), "tile", 1)
        from_right = shifted(jnp.concatenate([g_ul, g_ll]), "tile", -1)
        row_own = g_ul + from_left[:parts]
        row_right = g_ur + from_right[:parts]
        row_below = g_ll + from_left[parts:]
        row_corner = g_lr + from_right[parts:]
        from_above = shifted(jnp.concatenate([row_below, row_corner]), "tile", GRID)
        total_own = row_own + from_above[:parts]
        old_bands = lax.dynamic_slice_in_dim(quarters, chunk_start, chunk_rows, axis=2)
        probe_band_old = lax.dynamic_slice_in_dim(
            probe_modes.reshape(probe_parts, pattern_side, pattern_side), chunk_start, chunk_rows, axis=1
        )
        new_probe_band = probe_band_old - probe_step * probe_total
        if last:
            new_own = old_bands[0] - object_step * total_own
            full = gather_rows(jnp.concatenate([new_own, new_probe_band]), "scan")
            obj_state = full[:parts].reshape(obj_state.shape)
            probe_modes = full[parts:].reshape(probe_modes.shape)
        else:
            from_below = shifted(jnp.concatenate([row_own, row_right]), "tile", -GRID)
            totals = jnp.stack(
                [
                    total_own,
                    row_right + from_above[parts:],
                    row_below + from_below[:parts],
                    row_corner + from_below[parts:],
                ]
            )
            new_bands = old_bands - object_step * totals
            full = gather_rows(
                jnp.concatenate([new_bands.reshape(4 * parts, chunk_rows, block_side), new_probe_band]),
                "scan",
            )
            quarters = full[: 4 * parts].reshape(quarters.shape)
            probe_modes = full[4 * parts :].reshape(probe_modes.shape)
    return (obj_state[0][:, None], obj_state[1][:, None], probe_modes)


def solution(mesh):
    placed = (
        P(None, "tile", None, None),
        P(None, "tile", None, None),
        P(),
        P("tile", "scan", None, None, None),
        P("tile", "scan", None, None),
        P("tile", "scan", None),
    )
    return jax.shard_map(
        local,
        mesh=mesh,
        in_specs=placed,
        out_specs=(P(None, "tile", None, None), P(None, "tile", None, None), P()),
        check_vma=False,
    )
```

```python
import math

import jax
import jax.numpy as jnp
from jax import lax
from jax.experimental import pallas as pl
from jax.experimental.pallas import tpu as pltpu
from jax.sharding import PartitionSpec as P

GRID = 8
ITERS = 2


object_rate = 0.008
probe_rate = 0.03


def shifted(shard, axis, by):
    size = lax.axis_size(axis)
    return lax.ppermute(shard, axis, [(i, (i + by) % size) for i in range(size)])


def make_tables(pattern_side):
    positions = lax.iota(jnp.int32, pattern_side)
    product = positions[:, None] * positions[None, :] % pattern_side
    angles = 2.0 * math.pi / pattern_side * product.astype(jnp.float32)
    scaling = 1.0 / math.sqrt(pattern_side)
    frequency = jnp.where(
        positions < pattern_side // 2, positions, positions - pattern_side
    ).astype(jnp.float32)
    phases = (
        -4.0
        * math.pi
        * (frequency[:, None] ** 2 + frequency[None, :] ** 2)
        / (pattern_side * pattern_side)
    )
    return (jnp.cos(angles) * scaling, jnp.sin(angles) * scaling, jnp.cos(phases), jnp.sin(phases))


def from_left(matrix, values):
    return jnp.einsum("jk,mkl->mjl", matrix, values, precision=lax.Precision.HIGHEST)


def from_right(values, matrix):
    return jnp.einsum("mjk,kl->mjl", values, matrix, precision=lax.Precision.HIGHEST)


def transform(part_real, part_imag, tables, sign):
    cosine, sine_table = (tables[0], tables[1])
    left_real = from_left(cosine, part_real) + sign * from_left(sine_table, part_imag)
    left_imag = from_left(cosine, part_imag) - sign * from_left(sine_table, part_real)
    out_real = from_right(left_real, cosine) + sign * from_right(left_imag, sine_table)
    out_imag = from_right(left_imag, cosine) - sign * from_right(left_real, sine_table)
    return (out_real, out_imag)


def slot_loss(patch_cells, mode_values, target, weight, tables):
    depth_count = patch_cells.shape[1]
    wave_real, wave_imag = (mode_values[:, 0], mode_values[:, 1])
    for depth_index in range(depth_count):
        cell_real = patch_cells[0, depth_index]
        cell_imag = patch_cells[1, depth_index]
        wave_real, wave_imag = (
            wave_real * cell_real - wave_imag * cell_imag,
            wave_real * cell_imag + wave_imag * cell_real,
        )
        if depth_index < depth_count - 1:
            freq_real, freq_imag = transform(wave_real, wave_imag, tables, 1.0)
            kern_real, kern_imag = (tables[2], tables[3])
            freq_real, freq_imag = (
                freq_real * kern_real - freq_imag * kern_imag,
                freq_real * kern_imag + freq_imag * kern_real,
            )
            wave_real, wave_imag = transform(freq_real, freq_imag, tables, -1.0)
    far_real, far_imag = transform(wave_real, wave_imag, tables, 1.0)
    intensity = jnp.sum(far_real**2 + far_imag**2, axis=0)
    return 0.5 * weight * jnp.sum((intensity - target) ** 2)


def slot_kernel(cells_ref, probe_ref, target_ref, weight_ref, tab_ref, gcells_ref, gprobe_ref):
    cosine, sine_table, kern_real, kern_imag = (tab_ref[0], tab_ref[1], tab_ref[2], tab_ref[3])

    def dot(a, b):
        return jnp.dot(a, b, precision=lax.Precision.HIGHEST, preferred_element_type=jnp.float32)

    def forward(xr, xi):
        lr = dot(cosine, xr) + dot(sine_table, xi)
        li = dot(cosine, xi) - dot(sine_table, xr)
        return (dot(lr, cosine) + dot(li, sine_table), dot(li, cosine) - dot(lr, sine_table))

    def inverse(xr, xi):
        lr = dot(cosine, xr) - dot(sine_table, xi)
        li = dot(cosine, xi) + dot(sine_table, xr)
        return (dot(lr, cosine) - dot(li, sine_table), dot(li, cosine) + dot(lr, sine_table))

    def mul(a, b):
        return (a[0] * b[0] - a[1] * b[1], a[0] * b[1] + a[1] * b[0])

    def mul_conj(a, b):
        return (a[0] * b[0] + a[1] * b[1], a[1] * b[0] - a[0] * b[1])

    kern = (kern_real, kern_imag)
    propagate = lambda x: inverse(*mul(forward(*x), kern))
    propagate_adjoint = lambda x: inverse(*mul_conj(forward(*x), kern))
    depth_count = cells_ref.shape[1]
    mode_count = probe_ref.shape[0]
    layers = [(cells_ref[0, d], cells_ref[1, d]) for d in range(depth_count)]
    saved = []
    intensity = None
    for m in range(mode_count):
        wave = (probe_ref[m, 0], probe_ref[m, 1])
        inputs = []
        for d in range(depth_count):
            inputs.append(wave)
            wave = mul(wave, layers[d])
            if d < depth_count - 1:
                wave = propagate(wave)
        far = forward(*wave)
        saved.append((inputs, far))
        power = far[0] * far[0] + far[1] * far[1]
        intensity = power if intensity is None else intensity + power
    residual = weight_ref[...] * (intensity - target_ref[...])
    layer_grads = [None] * depth_count
    for m in range(mode_count):
        inputs, far = saved[m]
        grad = inverse(2.0 * residual * far[0], 2.0 * residual * far[1])
        for d in reversed(range(depth_count)):
            term = mul_conj(grad, inputs[d])
            if layer_grads[d] is None:
                layer_grads[d] = term
            else:
                layer_grads[d] = (layer_grads[d][0] + term[0], layer_grads[d][1] + term[1])
            grad = mul_conj(grad, layers[d])
            if d > 0:
                grad = propagate_adjoint(grad)
        gprobe_ref[m, 0] = grad[0]
        gprobe_ref[m, 1] = grad[1]
    for d in range(depth_count):
        gcells_ref[0, d] = layer_grads[d][0]
        gcells_ref[1, d] = layer_grads[d][1]


def slot_grad(patch_cells, mode_values, target, weight, tables):
    tab = jnp.stack(tables)
    side = target.shape[-1]
    dots = 2 * mode_values.shape[0] * 10 * 8
    return pl.pallas_call(
        slot_kernel,
        out_shape=(
            jax.ShapeDtypeStruct(patch_cells.shape, jnp.float32),
            jax.ShapeDtypeStruct(mode_values.shape, jnp.float32),
        ),
        in_specs=[pl.BlockSpec(memory_space=pltpu.VMEM)] * 5,
        out_specs=(pl.BlockSpec(memory_space=pltpu.VMEM), pl.BlockSpec(memory_space=pltpu.VMEM)),
        cost_estimate=pl.CostEstimate(
            flops=dots * 2 * side**3, bytes_accessed=4 * side * side * 22, transcendentals=0
        ),
    )(patch_cells, mode_values, target, weight.reshape(1, 1), tab)


def xor_sum(values, axis, steps=None):
    size = lax.axis_size(axis)
    if steps is None:
        steps = [1 << bit for bit in range(size.bit_length() - 1)]
    for step in steps:
        values = values + lax.ppermute(values, axis, [(i, i ^ step) for i in range(size)])
    return values


def a2a_sum(values, axis):
    size = lax.axis_size(axis)
    flat = values.reshape(size, -1)
    part = jnp.sum(lax.all_to_all(flat, axis, 0, 0, tiled=True), axis=0, keepdims=True)
    spread = lax.all_to_all(jnp.broadcast_to(part, flat.shape), axis, 0, 0, tiled=True)
    return spread.reshape(values.shape)


def local(object_real, object_imag, probe_modes, measured, offsets, live):
    slices = object_real.shape[0]
    block_side = object_real.shape[2]
    pattern_side = probe_modes.shape[2]
    slot_count = measured.shape[2]
    tile_count = lax.axis_size("tile")
    group_count = lax.axis_size("scan")
    tables = make_tables(pattern_side)
    anchor = jnp.zeros((), jnp.int32)
    obj_state = jnp.stack([object_real[:, 0], object_imag[:, 0]])
    parts = 2 * slices
    tile_bits = [1 << bit for bit in range(tile_count.bit_length() - 1)]
    first_bits = [b for b in tile_bits if b < GRID]
    second_bits = [b for b in tile_bits if b >= GRID]
    pending = None
    for iteration in range(ITERS + 1):
        if pending is not None:
            probe_sum = pending
            probe_modes = (
                probe_modes - probe_rate / (slot_count * tile_count * group_count) * probe_sum
            )
        if iteration == ITERS:
            break
        right_part = shifted(obj_state, "tile", -1)
        upper_half = jnp.concatenate([obj_state, right_part], axis=-1)
        lower_half = shifted(upper_half, "tile", -GRID)
        canvas = jnp.concatenate([upper_half, lower_half], axis=-2)
        current_probe = probe_modes

        grad_canvas = jnp.zeros_like(canvas)
        grad_probe = jnp.zeros_like(probe_modes)
        for slot_index in range(slot_count):
            row_start = offsets[0, 0, slot_index, 0]
            col_start = offsets[0, 0, slot_index, 1]
            starts = (anchor, anchor, row_start, col_start)
            patch_cells = lax.dynamic_slice(canvas, starts, (2, slices, pattern_side, pattern_side))
            target = measured[0, 0, slot_index]
            weight = live[0, 0, slot_index].astype(jnp.float32)
            grad_patch, grad_modes = slot_grad(patch_cells, current_probe, target, weight, tables)
            current = lax.dynamic_slice(
                grad_canvas, starts, (2, slices, pattern_side, pattern_side)
            )
            grad_canvas = lax.dynamic_update_slice(grad_canvas, current + grad_patch, starts)
            grad_probe = grad_probe + grad_modes
        planes = lambda a: a.reshape(-1, block_side, block_side)
        sent_down = jnp.concatenate(
            [
                planes(grad_canvas[:, :, block_side:, :block_side]),
                planes(grad_canvas[:, :, block_side:, block_side:]),
            ]
        )
        pair = lambda a, b: lax.optimization_barrier((a, b))
        probe_partial = xor_sum(grad_probe, "scan", [1])
        sent_down, probe_partial = pair(sent_down, probe_partial)
        came_down = shifted(sent_down, "tile", GRID)
        probe_partial = xor_sum(probe_partial, "scan", [2])
        own_part = planes(grad_canvas[:, :, :block_side, :block_side]) + came_down[:parts]
        right_side = planes(grad_canvas[:, :, :block_side, block_side:]) + came_down[parts:]
        right_side, probe_partial = pair(right_side, probe_partial)
        came_left = shifted(right_side, "tile", 1)
        probe_partial = xor_sum(probe_partial, "scan", [4])
        own_part = own_part + came_left
        own_part, probe_partial = pair(own_part, probe_partial)
        probe_partial = a2a_sum(probe_partial, "tile")
        own_part = xor_sum(own_part, "scan", [1, 2])
        own_part, probe_partial = pair(own_part, probe_partial)
        grad_total = xor_sum(own_part, "scan", [4]).reshape(obj_state.shape)
        pending = probe_partial
        obj_state = obj_state - object_rate / (slot_count * group_count) * grad_total
    return (obj_state[0][:, None], obj_state[1][:, None], probe_modes)


def solution(mesh):
    placed = (
        P(None, "tile", None, None),
        P(None, "tile", None, None),
        P(),
        P("tile", "scan", None, None, None),
        P("tile", "scan", None, None),
        P("tile", "scan", None),
    )
    return jax.shard_map(
        local,
        mesh=mesh,
        in_specs=placed,
        out_specs=(P(None, "tile", None, None), P(None, "tile", None, None), P()),
        check_vma=False,
    )
```

```python
import math

import jax
import jax.numpy as jnp
from jax import lax
from jax.experimental import pallas as pl
from jax.experimental.pallas import tpu as pltpu
from jax.sharding import PartitionSpec as P

GRID = 8
ITERS = 2


object_rate = 0.008
probe_rate = 0.03


def shifted(shard, axis, by):
    size = lax.axis_size(axis)
    return lax.ppermute(shard, axis, [(i, (i + by) % size) for i in range(size)])


def make_tables(pattern_side):
    positions = lax.iota(jnp.int32, pattern_side)
    product = positions[:, None] * positions[None, :] % pattern_side
    angles = 2.0 * math.pi / pattern_side * product.astype(jnp.float32)
    scaling = 1.0 / math.sqrt(pattern_side)
    frequency = jnp.where(
        positions < pattern_side // 2, positions, positions - pattern_side
    ).astype(jnp.float32)
    phases = (
        -4.0
        * math.pi
        * (frequency[:, None] ** 2 + frequency[None, :] ** 2)
        / (pattern_side * pattern_side)
    )
    return (jnp.cos(angles) * scaling, jnp.sin(angles) * scaling, jnp.cos(phases), jnp.sin(phases))


def from_left(matrix, values):
    return jnp.einsum("jk,mkl->mjl", matrix, values, precision=lax.Precision.HIGHEST)


def from_right(values, matrix):
    return jnp.einsum("mjk,kl->mjl", values, matrix, precision=lax.Precision.HIGHEST)


def transform(part_real, part_imag, tables, sign):
    cosine, sine_table = (tables[0], tables[1])
    left_real = from_left(cosine, part_real) + sign * from_left(sine_table, part_imag)
    left_imag = from_left(cosine, part_imag) - sign * from_left(sine_table, part_real)
    out_real = from_right(left_real, cosine) + sign * from_right(left_imag, sine_table)
    out_imag = from_right(left_imag, cosine) - sign * from_right(left_real, sine_table)
    return (out_real, out_imag)


def slot_loss(patch_cells, mode_values, target, weight, tables):
    depth_count = patch_cells.shape[1]
    wave_real, wave_imag = (mode_values[:, 0], mode_values[:, 1])
    for depth_index in range(depth_count):
        cell_real = patch_cells[0, depth_index]
        cell_imag = patch_cells[1, depth_index]
        wave_real, wave_imag = (
            wave_real * cell_real - wave_imag * cell_imag,
            wave_real * cell_imag + wave_imag * cell_real,
        )
        if depth_index < depth_count - 1:
            freq_real, freq_imag = transform(wave_real, wave_imag, tables, 1.0)
            kern_real, kern_imag = (tables[2], tables[3])
            freq_real, freq_imag = (
                freq_real * kern_real - freq_imag * kern_imag,
                freq_real * kern_imag + freq_imag * kern_real,
            )
            wave_real, wave_imag = transform(freq_real, freq_imag, tables, -1.0)
    far_real, far_imag = transform(wave_real, wave_imag, tables, 1.0)
    intensity = jnp.sum(far_real**2 + far_imag**2, axis=0)
    return 0.5 * weight * jnp.sum((intensity - target) ** 2)


def slot_kernel(cells_ref, probe_ref, target_ref, weight_ref, tab_ref, gcells_ref, gprobe_ref):
    side = target_ref.shape[0]
    mode_count = probe_ref.shape[0]
    depth_count = cells_ref.shape[1]
    wide = lambda a: jnp.concatenate([a] * mode_count, axis=1)
    cosine, sine_table = (tab_ref[0], tab_ref[1])
    kern = (wide(tab_ref[2]), wide(tab_ref[3]))
    zero = jnp.zeros_like(cosine)

    def block(a):
        rows = [
            jnp.concatenate([a if j == i else zero for j in range(mode_count)], axis=1)
            for i in range(mode_count)
        ]
        return jnp.concatenate(rows, axis=0)

    cos_block, sin_block = (block(cosine), block(sine_table))

    def dot(a, b):
        return jnp.dot(a, b, precision=lax.Precision.HIGHEST, preferred_element_type=jnp.float32)

    def forward(xr, xi):
        lr = dot(cosine, xr) + dot(sine_table, xi)
        li = dot(cosine, xi) - dot(sine_table, xr)
        return (dot(lr, cos_block) + dot(li, sin_block), dot(li, cos_block) - dot(lr, sin_block))

    def inverse(xr, xi):
        lr = dot(cosine, xr) - dot(sine_table, xi)
        li = dot(cosine, xi) + dot(sine_table, xr)
        return (dot(lr, cos_block) - dot(li, sin_block), dot(li, cos_block) + dot(lr, sin_block))

    def mul(a, b):
        return (a[0] * b[0] - a[1] * b[1], a[0] * b[1] + a[1] * b[0])

    def mul_conj(a, b):
        return (a[0] * b[0] + a[1] * b[1], a[1] * b[0] - a[0] * b[1])

    def fold(a):
        total = a[:, :side]
        for m in range(1, mode_count):
            total = total + a[:, m * side : (m + 1) * side]
        return total

    propagate = lambda x: inverse(*mul(forward(*x), kern))
    propagate_adjoint = lambda x: inverse(*mul_conj(forward(*x), kern))
    layers = [(wide(cells_ref[0, d]), wide(cells_ref[1, d])) for d in range(depth_count)]
    wave = (
        jnp.concatenate([probe_ref[m, 0] for m in range(mode_count)], axis=1),
        jnp.concatenate([probe_ref[m, 1] for m in range(mode_count)], axis=1),
    )
    inputs = []
    for d in range(depth_count):
        inputs.append(wave)
        wave = mul(wave, layers[d])
        if d < depth_count - 1:
            wave = propagate(wave)
    far = forward(*wave)
    intensity = fold(far[0] * far[0] + far[1] * far[1])
    residual = wide(weight_ref[...] * (intensity - target_ref[...]))
    grad = inverse(2.0 * residual * far[0], 2.0 * residual * far[1])
    for d in reversed(range(depth_count)):
        term = mul_conj(grad, inputs[d])
        gcells_ref[0, d] = fold(term[0])
        gcells_ref[1, d] = fold(term[1])
        grad = mul_conj(grad, layers[d])
        if d > 0:
            grad = propagate_adjoint(grad)
    for m in range(mode_count):
        gprobe_ref[m, 0] = grad[0][:, m * side : (m + 1) * side]
        gprobe_ref[m, 1] = grad[1][:, m * side : (m + 1) * side]


def slot_grad(patch_cells, mode_values, target, weight, tables):
    tab = jnp.stack(tables)
    side = target.shape[-1]
    dots = 2 * mode_values.shape[0] * 10 * 8
    return pl.pallas_call(
        slot_kernel,
        out_shape=(
            jax.ShapeDtypeStruct(patch_cells.shape, jnp.float32),
            jax.ShapeDtypeStruct(mode_values.shape, jnp.float32),
        ),
        in_specs=[pl.BlockSpec(memory_space=pltpu.VMEM)] * 5,
        out_specs=(pl.BlockSpec(memory_space=pltpu.VMEM), pl.BlockSpec(memory_space=pltpu.VMEM)),
        cost_estimate=pl.CostEstimate(
            flops=dots * 2 * side**3, bytes_accessed=4 * side * side * 22, transcendentals=0
        ),
    )(patch_cells, mode_values, target, weight.reshape(1, 1), tab)


def xor_sum(values, axis, steps=None):
    size = lax.axis_size(axis)
    if steps is None:
        steps = [1 << bit for bit in range(size.bit_length() - 1)]
    for step in steps:
        values = values + lax.ppermute(values, axis, [(i, i ^ step) for i in range(size)])
    return values


def a2a_sum(values, axis):
    size = lax.axis_size(axis)
    flat = values.reshape(size, -1)
    part = jnp.sum(lax.all_to_all(flat, axis, 0, 0, tiled=True), axis=0, keepdims=True)
    spread = lax.all_to_all(jnp.broadcast_to(part, flat.shape), axis, 0, 0, tiled=True)
    return spread.reshape(values.shape)


def local(object_real, object_imag, probe_modes, measured, offsets, live):
    slices = object_real.shape[0]
    block_side = object_real.shape[2]
    pattern_side = probe_modes.shape[2]
    slot_count = measured.shape[2]
    tile_count = lax.axis_size("tile")
    group_count = lax.axis_size("scan")
    tables = make_tables(pattern_side)
    anchor = jnp.zeros((), jnp.int32)
    obj_state = jnp.stack([object_real[:, 0], object_imag[:, 0]])
    parts = 2 * slices
    tile_bits = [1 << bit for bit in range(tile_count.bit_length() - 1)]
    first_bits = [b for b in tile_bits if b < GRID]
    second_bits = [b for b in tile_bits if b >= GRID]
    pending = None
    for iteration in range(ITERS + 1):
        if pending is not None:
            probe_sum = pending
            probe_modes = (
                probe_modes - probe_rate / (slot_count * tile_count * group_count) * probe_sum
            )
        if iteration == ITERS:
            break
        right_part = shifted(obj_state, "tile", -1)
        upper_half = jnp.concatenate([obj_state, right_part], axis=-1)
        lower_half = shifted(upper_half, "tile", -GRID)
        canvas = jnp.concatenate([upper_half, lower_half], axis=-2)
        current_probe = probe_modes

        grad_canvas = jnp.zeros_like(canvas)
        grad_probe = jnp.zeros_like(probe_modes)
        for slot_index in range(slot_count):
            row_start = offsets[0, 0, slot_index, 0]
            col_start = offsets[0, 0, slot_index, 1]
            starts = (anchor, anchor, row_start, col_start)
            patch_cells = lax.dynamic_slice(canvas, starts, (2, slices, pattern_side, pattern_side))
            target = measured[0, 0, slot_index]
            weight = live[0, 0, slot_index].astype(jnp.float32)
            grad_patch, grad_modes = slot_grad(patch_cells, current_probe, target, weight, tables)
            current = lax.dynamic_slice(
                grad_canvas, starts, (2, slices, pattern_side, pattern_side)
            )
            grad_canvas = lax.dynamic_update_slice(grad_canvas, current + grad_patch, starts)
            grad_probe = grad_probe + grad_modes
        planes = lambda a: a.reshape(-1, block_side, block_side)
        probe_partial = a2a_sum(xor_sum(grad_probe, "scan"), "tile")
        sent_down = jnp.concatenate(
            [
                planes(grad_canvas[:, :, block_side:, :block_side]),
                planes(grad_canvas[:, :, block_side:, block_side:]),
            ]
        )
        came_down = shifted(sent_down, "tile", GRID)
        own_part = planes(grad_canvas[:, :, :block_side, :block_side]) + came_down[:parts]
        right_side = planes(grad_canvas[:, :, :block_side, block_side:]) + came_down[parts:]
        own_part = own_part + shifted(right_side, "tile", 1)
        grad_total = xor_sum(own_part, "scan").reshape(obj_state.shape)
        pending = probe_partial
        obj_state = obj_state - object_rate / (slot_count * group_count) * grad_total
    return (obj_state[0][:, None], obj_state[1][:, None], probe_modes)


def solution(mesh):
    placed = (
        P(None, "tile", None, None),
        P(None, "tile", None, None),
        P(),
        P("tile", "scan", None, None, None),
        P("tile", "scan", None, None),
        P("tile", "scan", None),
    )
    return jax.shard_map(
        local,
        mesh=mesh,
        in_specs=placed,
        out_specs=(P(None, "tile", None, None), P(None, "tile", None, None), P()),
        check_vma=False,
    )
```

```python
import math

import jax
import jax.numpy as jnp
from jax import lax
from jax.experimental import pallas as pl
from jax.experimental.pallas import tpu as pltpu
from jax.sharding import PartitionSpec as P

GRID = 8
ITERS = 2


object_rate = 0.008
probe_rate = 0.03


def shifted(shard, axis, by):
    size = lax.axis_size(axis)
    return lax.ppermute(shard, axis, [(i, (i + by) % size) for i in range(size)])


def make_tables(pattern_side):
    positions = lax.iota(jnp.int32, pattern_side)
    product = positions[:, None] * positions[None, :] % pattern_side
    angles = 2.0 * math.pi / pattern_side * product.astype(jnp.float32)
    scaling = 1.0 / math.sqrt(pattern_side)
    frequency = jnp.where(
        positions < pattern_side // 2, positions, positions - pattern_side
    ).astype(jnp.float32)
    phases = (
        -4.0
        * math.pi
        * (frequency[:, None] ** 2 + frequency[None, :] ** 2)
        / (pattern_side * pattern_side)
    )
    return (jnp.cos(angles) * scaling, jnp.sin(angles) * scaling, jnp.cos(phases), jnp.sin(phases))


def from_left(matrix, values):
    return jnp.einsum("jk,mkl->mjl", matrix, values, precision=lax.Precision.HIGHEST)


def from_right(values, matrix):
    return jnp.einsum("mjk,kl->mjl", values, matrix, precision=lax.Precision.HIGHEST)


def transform(part_real, part_imag, tables, sign):
    cosine, sine_table = (tables[0], tables[1])
    left_real = from_left(cosine, part_real) + sign * from_left(sine_table, part_imag)
    left_imag = from_left(cosine, part_imag) - sign * from_left(sine_table, part_real)
    out_real = from_right(left_real, cosine) + sign * from_right(left_imag, sine_table)
    out_imag = from_right(left_imag, cosine) - sign * from_right(left_real, sine_table)
    return (out_real, out_imag)


def slot_loss(patch_cells, mode_values, target, weight, tables):
    depth_count = patch_cells.shape[1]
    wave_real, wave_imag = (mode_values[:, 0], mode_values[:, 1])
    for depth_index in range(depth_count):
        cell_real = patch_cells[0, depth_index]
        cell_imag = patch_cells[1, depth_index]
        wave_real, wave_imag = (
            wave_real * cell_real - wave_imag * cell_imag,
            wave_real * cell_imag + wave_imag * cell_real,
        )
        if depth_index < depth_count - 1:
            freq_real, freq_imag = transform(wave_real, wave_imag, tables, 1.0)
            kern_real, kern_imag = (tables[2], tables[3])
            freq_real, freq_imag = (
                freq_real * kern_real - freq_imag * kern_imag,
                freq_real * kern_imag + freq_imag * kern_real,
            )
            wave_real, wave_imag = transform(freq_real, freq_imag, tables, -1.0)
    far_real, far_imag = transform(wave_real, wave_imag, tables, 1.0)
    intensity = jnp.sum(far_real**2 + far_imag**2, axis=0)
    return 0.5 * weight * jnp.sum((intensity - target) ** 2)


def slot_kernel(cells_ref, probe_ref, target_ref, weight_ref, tab_ref, gcells_ref, gprobe_ref):
    side = target_ref.shape[0]
    mode_count = probe_ref.shape[0]
    depth_count = cells_ref.shape[1]
    wide = lambda a: jnp.concatenate([a] * mode_count, axis=1)
    cosine, sine_table = (tab_ref[0], tab_ref[1])
    kern = (wide(tab_ref[2]), wide(tab_ref[3]))
    zero = jnp.zeros_like(cosine)

    def block(a):
        rows = [
            jnp.concatenate([a if j == i else zero for j in range(mode_count)], axis=1)
            for i in range(mode_count)
        ]
        return jnp.concatenate(rows, axis=0)

    cos_block, sin_block = (block(cosine), block(sine_table))

    def dot(a, b):
        return jnp.dot(a, b, precision=lax.Precision.HIGHEST, preferred_element_type=jnp.float32)

    def forward(xr, xi):
        lr = dot(cosine, xr) + dot(sine_table, xi)
        li = dot(cosine, xi) - dot(sine_table, xr)
        return (dot(lr, cos_block) + dot(li, sin_block), dot(li, cos_block) - dot(lr, sin_block))

    def inverse(xr, xi):
        lr = dot(cosine, xr) - dot(sine_table, xi)
        li = dot(cosine, xi) + dot(sine_table, xr)
        return (dot(lr, cos_block) - dot(li, sin_block), dot(li, cos_block) + dot(lr, sin_block))

    def mul(a, b):
        return (a[0] * b[0] - a[1] * b[1], a[0] * b[1] + a[1] * b[0])

    def mul_conj(a, b):
        return (a[0] * b[0] + a[1] * b[1], a[1] * b[0] - a[0] * b[1])

    def fold(a):
        total = a[:, :side]
        for m in range(1, mode_count):
            total = total + a[:, m * side : (m + 1) * side]
        return total

    propagate = lambda x: inverse(*mul(forward(*x), kern))
    propagate_adjoint = lambda x: inverse(*mul_conj(forward(*x), kern))
    layers = [(wide(cells_ref[0, d]), wide(cells_ref[1, d])) for d in range(depth_count)]
    wave = (
        jnp.concatenate([probe_ref[m, 0] for m in range(mode_count)], axis=1),
        jnp.concatenate([probe_ref[m, 1] for m in range(mode_count)], axis=1),
    )
    inputs = []
    for d in range(depth_count):
        inputs.append(wave)
        wave = mul(wave, layers[d])
        if d < depth_count - 1:
            wave = propagate(wave)
    far = forward(*wave)
    intensity = fold(far[0] * far[0] + far[1] * far[1])
    residual = wide(weight_ref[...] * (intensity - target_ref[...]))
    grad = inverse(2.0 * residual * far[0], 2.0 * residual * far[1])
    for d in reversed(range(depth_count)):
        term = mul_conj(grad, inputs[d])
        gcells_ref[0, d] = fold(term[0])
        gcells_ref[1, d] = fold(term[1])
        grad = mul_conj(grad, layers[d])
        if d > 0:
            grad = propagate_adjoint(grad)
    for m in range(mode_count):
        gprobe_ref[m, 0] = grad[0][:, m * side : (m + 1) * side]
        gprobe_ref[m, 1] = grad[1][:, m * side : (m + 1) * side]


def slot_grad(patch_cells, mode_values, target, weight, tables):
    tab = jnp.stack(tables)
    side = target.shape[-1]
    dots = 2 * mode_values.shape[0] * 10 * 8
    return pl.pallas_call(
        slot_kernel,
        out_shape=(
            jax.ShapeDtypeStruct(patch_cells.shape, jnp.float32),
            jax.ShapeDtypeStruct(mode_values.shape, jnp.float32),
        ),
        in_specs=[pl.BlockSpec(memory_space=pltpu.VMEM)] * 5,
        out_specs=(pl.BlockSpec(memory_space=pltpu.VMEM), pl.BlockSpec(memory_space=pltpu.VMEM)),
        cost_estimate=pl.CostEstimate(
            flops=dots * 2 * side**3, bytes_accessed=4 * side * side * 22, transcendentals=0
        ),
    )(patch_cells, mode_values, target, weight.reshape(1, 1), tab)


def xor_sum(values, axis, steps=None):
    size = lax.axis_size(axis)
    if steps is None:
        steps = [1 << bit for bit in range(size.bit_length() - 1)]
    for step in steps:
        values = values + lax.ppermute(values, axis, [(i, i ^ step) for i in range(size)])
    return values


def a2a_sum(values, axis):
    size = lax.axis_size(axis)
    flat = values.reshape(size, -1)
    part = jnp.sum(lax.all_to_all(flat, axis, 0, 0, tiled=True), axis=0, keepdims=True)
    spread = lax.all_to_all(jnp.broadcast_to(part, flat.shape), axis, 0, 0, tiled=True)
    return spread.reshape(values.shape)


def local(object_real, object_imag, probe_modes, measured, offsets, live):
    slices = object_real.shape[0]
    block_side = object_real.shape[2]
    pattern_side = probe_modes.shape[2]
    slot_count = measured.shape[2]
    tile_count = lax.axis_size("tile")
    group_count = lax.axis_size("scan")
    tables = make_tables(pattern_side)
    anchor = jnp.zeros((), jnp.int32)
    obj_state = jnp.stack([object_real[:, 0], object_imag[:, 0]])
    parts = 2 * slices
    tile_bits = [1 << bit for bit in range(tile_count.bit_length() - 1)]
    first_bits = [b for b in tile_bits if b < GRID]
    second_bits = [b for b in tile_bits if b >= GRID]
    pending = None
    for iteration in range(ITERS + 1):
        if pending is not None:
            probe_sum = pending
            probe_modes = (
                probe_modes - probe_rate / (slot_count * tile_count * group_count) * probe_sum
            )
        if iteration == ITERS:
            break
        right_part = shifted(obj_state, "tile", -1)
        upper_half = jnp.concatenate([obj_state, right_part], axis=-1)
        lower_half = shifted(upper_half, "tile", -GRID)
        canvas = jnp.concatenate([upper_half, lower_half], axis=-2)
        current_probe = probe_modes

        grad_canvas = jnp.zeros_like(canvas)
        grad_probe = jnp.zeros_like(probe_modes)
        for slot_index in range(slot_count):
            row_start = offsets[0, 0, slot_index, 0]
            col_start = offsets[0, 0, slot_index, 1]
            starts = (anchor, anchor, row_start, col_start)
            patch_cells = lax.dynamic_slice(canvas, starts, (2, slices, pattern_side, pattern_side))
            target = measured[0, 0, slot_index]
            weight = live[0, 0, slot_index].astype(jnp.float32)
            grad_patch, grad_modes = slot_grad(patch_cells, current_probe, target, weight, tables)
            current = lax.dynamic_slice(
                grad_canvas, starts, (2, slices, pattern_side, pattern_side)
            )
            grad_canvas = lax.dynamic_update_slice(grad_canvas, current + grad_patch, starts)
            grad_probe = grad_probe + grad_modes
        if slot_count == 1 and pattern_side == block_side:
            spread = jnp.pad(
                grad_patch, ((0, 0), (0, 0), (block_side, block_side), (block_side, block_side))
            )
            quarter = lambda y0, x0: lax.dynamic_slice(
                spread,
                (anchor, anchor, y0 - row_start, x0 - col_start),
                (2, slices, block_side, block_side),
            )
            grad_ul, grad_ur = (quarter(block_side, block_side), quarter(block_side, 2 * block_side))
            grad_ll = quarter(2 * block_side, block_side)
            grad_lr = quarter(2 * block_side, 2 * block_side)
        else:
            grad_ul = grad_canvas[:, :, :block_side, :block_side]
            grad_ur = grad_canvas[:, :, :block_side, block_side:]
            grad_ll = grad_canvas[:, :, block_side:, :block_side]
            grad_lr = grad_canvas[:, :, block_side:, block_side:]
        planes = lambda a: a.reshape(-1, block_side, block_side)
        probe_partial = a2a_sum(xor_sum(grad_probe, "scan"), "tile")
        sent_down = jnp.concatenate(
            [
                planes(grad_ll),
                planes(grad_lr),
            ]
        )
        came_down = shifted(sent_down, "tile", GRID)
        own_part = planes(grad_ul) + came_down[:parts]
        right_side = planes(grad_ur) + came_down[parts:]
        own_part = own_part + shifted(right_side, "tile", 1)
        grad_total = xor_sum(own_part, "scan").reshape(obj_state.shape)
        pending = probe_partial
        obj_state = obj_state - object_rate / (slot_count * group_count) * grad_total
    return (obj_state[0][:, None], obj_state[1][:, None], probe_modes)


def solution(mesh):
    placed = (
        P(None, "tile", None, None),
        P(None, "tile", None, None),
        P(),
        P("tile", "scan", None, None, None),
        P("tile", "scan", None, None),
        P("tile", "scan", None),
    )
    return jax.shard_map(
        local,
        mesh=mesh,
        in_specs=placed,
        out_specs=(P(None, "tile", None, None), P(None, "tile", None, None), P()),
        check_vma=False,
    )
```

```python
import math

import jax
import jax.numpy as jnp
from jax import lax
from jax.experimental import pallas as pl
from jax.experimental.pallas import tpu as pltpu
from jax.sharding import PartitionSpec as P

GRID = 8
ITERS = 2


object_rate = 0.008
probe_rate = 0.03


def shifted(shard, axis, by):
    size = lax.axis_size(axis)
    return lax.ppermute(shard, axis, [(i, (i + by) % size) for i in range(size)])


def make_tables(pattern_side):
    positions = lax.iota(jnp.int32, pattern_side)
    product = positions[:, None] * positions[None, :] % pattern_side
    angles = 2.0 * math.pi / pattern_side * product.astype(jnp.float32)
    scaling = 1.0 / math.sqrt(pattern_side)
    frequency = jnp.where(
        positions < pattern_side // 2, positions, positions - pattern_side
    ).astype(jnp.float32)
    phases = (
        -4.0
        * math.pi
        * (frequency[:, None] ** 2 + frequency[None, :] ** 2)
        / (pattern_side * pattern_side)
    )
    return (jnp.cos(angles) * scaling, jnp.sin(angles) * scaling, jnp.cos(phases), jnp.sin(phases))


def from_left(matrix, values):
    return jnp.einsum("jk,mkl->mjl", matrix, values, precision=lax.Precision.HIGHEST)


def from_right(values, matrix):
    return jnp.einsum("mjk,kl->mjl", values, matrix, precision=lax.Precision.HIGHEST)


def transform(part_real, part_imag, tables, sign):
    cosine, sine_table = (tables[0], tables[1])
    left_real = from_left(cosine, part_real) + sign * from_left(sine_table, part_imag)
    left_imag = from_left(cosine, part_imag) - sign * from_left(sine_table, part_real)
    out_real = from_right(left_real, cosine) + sign * from_right(left_imag, sine_table)
    out_imag = from_right(left_imag, cosine) - sign * from_right(left_real, sine_table)
    return (out_real, out_imag)


def slot_loss(patch_cells, mode_values, target, weight, tables):
    depth_count = patch_cells.shape[1]
    wave_real, wave_imag = (mode_values[:, 0], mode_values[:, 1])
    for depth_index in range(depth_count):
        cell_real = patch_cells[0, depth_index]
        cell_imag = patch_cells[1, depth_index]
        wave_real, wave_imag = (
            wave_real * cell_real - wave_imag * cell_imag,
            wave_real * cell_imag + wave_imag * cell_real,
        )
        if depth_index < depth_count - 1:
            freq_real, freq_imag = transform(wave_real, wave_imag, tables, 1.0)
            kern_real, kern_imag = (tables[2], tables[3])
            freq_real, freq_imag = (
                freq_real * kern_real - freq_imag * kern_imag,
                freq_real * kern_imag + freq_imag * kern_real,
            )
            wave_real, wave_imag = transform(freq_real, freq_imag, tables, -1.0)
    far_real, far_imag = transform(wave_real, wave_imag, tables, 1.0)
    intensity = jnp.sum(far_real**2 + far_imag**2, axis=0)
    return 0.5 * weight * jnp.sum((intensity - target) ** 2)


def slot_kernel(cells_ref, probe_ref, target_ref, weight_ref, tab_ref, gcells_ref, gprobe_ref):
    side = target_ref.shape[0]
    mode_count = probe_ref.shape[0]
    depth_count = cells_ref.shape[1]
    wide = lambda a: jnp.concatenate([a] * mode_count, axis=1)
    cosine, sine_table = (tab_ref[0], tab_ref[1])
    kern = (wide(tab_ref[2]), wide(tab_ref[3]))
    zero = jnp.zeros_like(cosine)

    def block(a):
        rows = [
            jnp.concatenate([a if j == i else zero for j in range(mode_count)], axis=1)
            for i in range(mode_count)
        ]
        return jnp.concatenate(rows, axis=0)

    cos_block, sin_block = (block(cosine), block(sine_table))

    def dot(a, b):
        return jnp.dot(a, b, precision=lax.Precision.HIGHEST, preferred_element_type=jnp.float32)

    def forward(xr, xi):
        lr = dot(cosine, xr) + dot(sine_table, xi)
        li = dot(cosine, xi) - dot(sine_table, xr)
        return (dot(lr, cos_block) + dot(li, sin_block), dot(li, cos_block) - dot(lr, sin_block))

    def inverse(xr, xi):
        lr = dot(cosine, xr) - dot(sine_table, xi)
        li = dot(cosine, xi) + dot(sine_table, xr)
        return (dot(lr, cos_block) - dot(li, sin_block), dot(li, cos_block) + dot(lr, sin_block))

    def mul(a, b):
        return (a[0] * b[0] - a[1] * b[1], a[0] * b[1] + a[1] * b[0])

    def mul_conj(a, b):
        return (a[0] * b[0] + a[1] * b[1], a[1] * b[0] - a[0] * b[1])

    def fold(a):
        total = a[:, :side]
        for m in range(1, mode_count):
            total = total + a[:, m * side : (m + 1) * side]
        return total

    propagate = lambda x: inverse(*mul(forward(*x), kern))
    propagate_adjoint = lambda x: inverse(*mul_conj(forward(*x), kern))
    layers = [(wide(cells_ref[0, d]), wide(cells_ref[1, d])) for d in range(depth_count)]
    wave = (
        jnp.concatenate([probe_ref[m, 0] for m in range(mode_count)], axis=1),
        jnp.concatenate([probe_ref[m, 1] for m in range(mode_count)], axis=1),
    )
    inputs = []
    for d in range(depth_count):
        inputs.append(wave)
        wave = mul(wave, layers[d])
        if d < depth_count - 1:
            wave = propagate(wave)
    far = forward(*wave)
    intensity = fold(far[0] * far[0] + far[1] * far[1])
    residual = wide(weight_ref[...] * (intensity - target_ref[...]))
    grad = inverse(2.0 * residual * far[0], 2.0 * residual * far[1])
    for d in reversed(range(depth_count)):
        term = mul_conj(grad, inputs[d])
        gcells_ref[0, d] = fold(term[0])
        gcells_ref[1, d] = fold(term[1])
        grad = mul_conj(grad, layers[d])
        if d > 0:
            grad = propagate_adjoint(grad)
    for m in range(mode_count):
        gprobe_ref[m, 0] = grad[0][:, m * side : (m + 1) * side]
        gprobe_ref[m, 1] = grad[1][:, m * side : (m + 1) * side]


def slot_grad(patch_cells, mode_values, target, weight, tables):
    tab = jnp.stack(tables)
    side = target.shape[-1]
    dots = 2 * mode_values.shape[0] * 10 * 8
    return pl.pallas_call(
        slot_kernel,
        out_shape=(
            jax.ShapeDtypeStruct(patch_cells.shape, jnp.float32),
            jax.ShapeDtypeStruct(mode_values.shape, jnp.float32),
        ),
        in_specs=[pl.BlockSpec(memory_space=pltpu.VMEM)] * 5,
        out_specs=(pl.BlockSpec(memory_space=pltpu.VMEM), pl.BlockSpec(memory_space=pltpu.VMEM)),
        cost_estimate=pl.CostEstimate(
            flops=dots * 2 * side**3, bytes_accessed=4 * side * side * 22, transcendentals=0
        ),
    )(patch_cells, mode_values, target, weight.reshape(1, 1), tab)


def xor_sum(values, axis, steps=None):
    size = lax.axis_size(axis)
    if steps is None:
        steps = [1 << bit for bit in range(size.bit_length() - 1)]
    for step in steps:
        values = values + lax.ppermute(values, axis, [(i, i ^ step) for i in range(size)])
    return values


def a2a_sum(values, axis):
    size = lax.axis_size(axis)
    flat = values.reshape(size, -1)
    part = jnp.sum(lax.all_to_all(flat, axis, 0, 0, tiled=True), axis=0, keepdims=True)
    spread = lax.all_to_all(jnp.broadcast_to(part, flat.shape), axis, 0, 0, tiled=True)
    return spread.reshape(values.shape)


def local(object_real, object_imag, probe_modes, measured, offsets, live):
    slices = object_real.shape[0]
    block_side = object_real.shape[2]
    pattern_side = probe_modes.shape[2]
    slot_count = measured.shape[2]
    tile_count = lax.axis_size("tile")
    group_count = lax.axis_size("scan")
    tables = make_tables(pattern_side)
    anchor = jnp.zeros((), jnp.int32)
    obj_state = jnp.stack([object_real[:, 0], object_imag[:, 0]])
    parts = 2 * slices
    tile_bits = [1 << bit for bit in range(tile_count.bit_length() - 1)]
    first_bits = [b for b in tile_bits if b < GRID]
    second_bits = [b for b in tile_bits if b >= GRID]
    pending = None
    for iteration in range(ITERS + 1):
        if pending is not None:
            probe_sum = pending
            probe_modes = (
                probe_modes - probe_rate / (slot_count * tile_count * group_count) * probe_sum
            )
        if iteration == ITERS:
            break
        right_part = shifted(obj_state, "tile", -1)
        below_part = shifted(obj_state, "tile", -GRID)
        corner_part = shifted(below_part, "tile", -1)
        upper_half = jnp.concatenate([obj_state, right_part], axis=-1)
        lower_half = jnp.concatenate([below_part, corner_part], axis=-1)
        canvas = jnp.concatenate([upper_half, lower_half], axis=-2)
        current_probe = probe_modes

        grad_canvas = jnp.zeros_like(canvas)
        grad_probe = jnp.zeros_like(probe_modes)
        for slot_index in range(slot_count):
            row_start = offsets[0, 0, slot_index, 0]
            col_start = offsets[0, 0, slot_index, 1]
            starts = (anchor, anchor, row_start, col_start)
            patch_cells = lax.dynamic_slice(canvas, starts, (2, slices, pattern_side, pattern_side))
            target = measured[0, 0, slot_index]
            weight = live[0, 0, slot_index].astype(jnp.float32)
            grad_patch, grad_modes = slot_grad(patch_cells, current_probe, target, weight, tables)
            current = lax.dynamic_slice(
                grad_canvas, starts, (2, slices, pattern_side, pattern_side)
            )
            grad_canvas = lax.dynamic_update_slice(grad_canvas, current + grad_patch, starts)
            grad_probe = grad_probe + grad_modes
        if slot_count == 1 and pattern_side == block_side:
            spread = jnp.pad(
                grad_patch, ((0, 0), (0, 0), (block_side, block_side), (block_side, block_side))
            )
            quarter = lambda y0, x0: lax.dynamic_slice(
                spread,
                (anchor, anchor, y0 - row_start, x0 - col_start),
                (2, slices, block_side, block_side),
            )
            grad_ul, grad_ur = (quarter(block_side, block_side), quarter(block_side, 2 * block_side))
            grad_ll = quarter(2 * block_side, block_side)
            grad_lr = quarter(2 * block_side, 2 * block_side)
        else:
            grad_ul = grad_canvas[:, :, :block_side, :block_side]
            grad_ur = grad_canvas[:, :, :block_side, block_side:]
            grad_ll = grad_canvas[:, :, block_side:, :block_side]
            grad_lr = grad_canvas[:, :, block_side:, block_side:]
        planes = lambda a: a.reshape(-1, block_side, block_side)
        probe_partial = a2a_sum(xor_sum(grad_probe, "scan"), "tile")
        sent_down = jnp.concatenate(
            [
                planes(grad_ll),
                planes(grad_lr),
            ]
        )
        came_down = shifted(sent_down, "tile", GRID)
        own_part = planes(grad_ul) + came_down[:parts]
        right_side = planes(grad_ur) + came_down[parts:]
        own_part = own_part + shifted(right_side, "tile", 1)
        grad_total = xor_sum(own_part, "scan").reshape(obj_state.shape)
        pending = probe_partial
        obj_state = obj_state - object_rate / (slot_count * group_count) * grad_total
    return (obj_state[0][:, None], obj_state[1][:, None], probe_modes)


def solution(mesh):
    placed = (
        P(None, "tile", None, None),
        P(None, "tile", None, None),
        P(),
        P("tile", "scan", None, None, None),
        P("tile", "scan", None, None),
        P("tile", "scan", None),
    )
    return jax.shard_map(
        local,
        mesh=mesh,
        in_specs=placed,
        out_specs=(P(None, "tile", None, None), P(None, "tile", None, None), P()),
        check_vma=False,
    )
```

```python
import math

import jax
import jax.numpy as jnp
from jax import lax
from jax.experimental import pallas as pl
from jax.experimental.pallas import tpu as pltpu
from jax.sharding import PartitionSpec as P

GRID = 8
ITERS = 2


object_rate = 0.008
probe_rate = 0.03


def shifted(shard, axis, by):
    size = lax.axis_size(axis)
    return lax.ppermute(shard, axis, [(i, (i + by) % size) for i in range(size)])


def make_tables(pattern_side):
    positions = lax.iota(jnp.int32, pattern_side)
    product = positions[:, None] * positions[None, :] % pattern_side
    angles = 2.0 * math.pi / pattern_side * product.astype(jnp.float32)
    scaling = 1.0 / math.sqrt(pattern_side)
    frequency = jnp.where(
        positions < pattern_side // 2, positions, positions - pattern_side
    ).astype(jnp.float32)
    phases = (
        -4.0
        * math.pi
        * (frequency[:, None] ** 2 + frequency[None, :] ** 2)
        / (pattern_side * pattern_side)
    )
    return (jnp.cos(angles) * scaling, jnp.sin(angles) * scaling, jnp.cos(phases), jnp.sin(phases))


def from_left(matrix, values):
    return jnp.einsum("jk,mkl->mjl", matrix, values, precision=lax.Precision.HIGHEST)


def from_right(values, matrix):
    return jnp.einsum("mjk,kl->mjl", values, matrix, precision=lax.Precision.HIGHEST)


def transform(part_real, part_imag, tables, sign):
    cosine, sine_table = (tables[0], tables[1])
    left_real = from_left(cosine, part_real) + sign * from_left(sine_table, part_imag)
    left_imag = from_left(cosine, part_imag) - sign * from_left(sine_table, part_real)
    out_real = from_right(left_real, cosine) + sign * from_right(left_imag, sine_table)
    out_imag = from_right(left_imag, cosine) - sign * from_right(left_real, sine_table)
    return (out_real, out_imag)


def slot_loss(patch_cells, mode_values, target, weight, tables):
    depth_count = patch_cells.shape[1]
    wave_real, wave_imag = (mode_values[:, 0], mode_values[:, 1])
    for depth_index in range(depth_count):
        cell_real = patch_cells[0, depth_index]
        cell_imag = patch_cells[1, depth_index]
        wave_real, wave_imag = (
            wave_real * cell_real - wave_imag * cell_imag,
            wave_real * cell_imag + wave_imag * cell_real,
        )
        if depth_index < depth_count - 1:
            freq_real, freq_imag = transform(wave_real, wave_imag, tables, 1.0)
            kern_real, kern_imag = (tables[2], tables[3])
            freq_real, freq_imag = (
                freq_real * kern_real - freq_imag * kern_imag,
                freq_real * kern_imag + freq_imag * kern_real,
            )
            wave_real, wave_imag = transform(freq_real, freq_imag, tables, -1.0)
    far_real, far_imag = transform(wave_real, wave_imag, tables, 1.0)
    intensity = jnp.sum(far_real**2 + far_imag**2, axis=0)
    return 0.5 * weight * jnp.sum((intensity - target) ** 2)


def slot_kernel(cells_ref, probe_ref, target_ref, weight_ref, tab_ref, gcells_ref, gprobe_ref):
    side = target_ref.shape[0]
    mode_count = probe_ref.shape[0]
    depth_count = cells_ref.shape[1]
    wide = lambda a: jnp.concatenate([a] * mode_count, axis=1)
    cosine, sine_table = (tab_ref[0], tab_ref[1])
    kern = (wide(tab_ref[2]), wide(tab_ref[3]))

    stack = lambda a: jnp.concatenate(
        [a[:, m * side : (m + 1) * side] for m in range(mode_count)], axis=0
    )
    unstack = lambda a: jnp.concatenate(
        [a[m * side : (m + 1) * side] for m in range(mode_count)], axis=1
    )

    def dot(a, b):
        return jnp.dot(a, b, precision=lax.Precision.HIGHEST, preferred_element_type=jnp.float32)

    def forward(xr, xi):
        lr = dot(cosine, xr) + dot(sine_table, xi)
        li = dot(cosine, xi) - dot(sine_table, xr)
        lr, li = (stack(lr), stack(li))
        return (
            unstack(dot(lr, cosine) + dot(li, sine_table)),
            unstack(dot(li, cosine) - dot(lr, sine_table)),
        )

    def inverse(xr, xi):
        lr = dot(cosine, xr) - dot(sine_table, xi)
        li = dot(cosine, xi) + dot(sine_table, xr)
        lr, li = (stack(lr), stack(li))
        return (
            unstack(dot(lr, cosine) - dot(li, sine_table)),
            unstack(dot(li, cosine) + dot(lr, sine_table)),
        )

    def mul(a, b):
        return (a[0] * b[0] - a[1] * b[1], a[0] * b[1] + a[1] * b[0])

    def mul_conj(a, b):
        return (a[0] * b[0] + a[1] * b[1], a[1] * b[0] - a[0] * b[1])

    def fold(a):
        total = a[:, :side]
        for m in range(1, mode_count):
            total = total + a[:, m * side : (m + 1) * side]
        return total

    propagate = lambda x: inverse(*mul(forward(*x), kern))
    propagate_adjoint = lambda x: inverse(*mul_conj(forward(*x), kern))
    layers = [(wide(cells_ref[0, d]), wide(cells_ref[1, d])) for d in range(depth_count)]
    wave = (
        jnp.concatenate([probe_ref[m, 0] for m in range(mode_count)], axis=1),
        jnp.concatenate([probe_ref[m, 1] for m in range(mode_count)], axis=1),
    )
    inputs = []
    for d in range(depth_count):
        inputs.append(wave)
        wave = mul(wave, layers[d])
        if d < depth_count - 1:
            wave = propagate(wave)
    far = forward(*wave)
    intensity = fold(far[0] * far[0] + far[1] * far[1])
    residual = wide(weight_ref[...] * (intensity - target_ref[...]))
    grad = inverse(2.0 * residual * far[0], 2.0 * residual * far[1])
    for d in reversed(range(depth_count)):
        term = mul_conj(grad, inputs[d])
        gcells_ref[0, d] = fold(term[0])
        gcells_ref[1, d] = fold(term[1])
        grad = mul_conj(grad, layers[d])
        if d > 0:
            grad = propagate_adjoint(grad)
    for m in range(mode_count):
        gprobe_ref[m, 0] = grad[0][:, m * side : (m + 1) * side]
        gprobe_ref[m, 1] = grad[1][:, m * side : (m + 1) * side]


def slot_grad(patch_cells, mode_values, target, weight, tables):
    tab = jnp.stack(tables)
    side = target.shape[-1]
    dots = 2 * mode_values.shape[0] * 10 * 8
    return pl.pallas_call(
        slot_kernel,
        out_shape=(
            jax.ShapeDtypeStruct(patch_cells.shape, jnp.float32),
            jax.ShapeDtypeStruct(mode_values.shape, jnp.float32),
        ),
        in_specs=[pl.BlockSpec(memory_space=pltpu.VMEM)] * 5,
        out_specs=(pl.BlockSpec(memory_space=pltpu.VMEM), pl.BlockSpec(memory_space=pltpu.VMEM)),
        cost_estimate=pl.CostEstimate(
            flops=dots * 2 * side**3, bytes_accessed=4 * side * side * 22, transcendentals=0
        ),
    )(patch_cells, mode_values, target, weight.reshape(1, 1), tab)


def xor_sum(values, axis, steps=None):
    size = lax.axis_size(axis)
    if steps is None:
        steps = [1 << bit for bit in range(size.bit_length() - 1)]
    for step in steps:
        values = values + lax.ppermute(values, axis, [(i, i ^ step) for i in range(size)])
    return values


def a2a_sum(values, axis):
    size = lax.axis_size(axis)
    flat = values.reshape(size, -1)
    part = jnp.sum(lax.all_to_all(flat, axis, 0, 0, tiled=True), axis=0, keepdims=True)
    spread = lax.all_to_all(jnp.broadcast_to(part, flat.shape), axis, 0, 0, tiled=True)
    return spread.reshape(values.shape)


def local(object_real, object_imag, probe_modes, measured, offsets, live):
    slices = object_real.shape[0]
    block_side = object_real.shape[2]
    pattern_side = probe_modes.shape[2]
    slot_count = measured.shape[2]
    tile_count = lax.axis_size("tile")
    group_count = lax.axis_size("scan")
    tables = make_tables(pattern_side)
    anchor = jnp.zeros((), jnp.int32)
    obj_state = jnp.stack([object_real[:, 0], object_imag[:, 0]])
    parts = 2 * slices
    tile_bits = [1 << bit for bit in range(tile_count.bit_length() - 1)]
    first_bits = [b for b in tile_bits if b < GRID]
    second_bits = [b for b in tile_bits if b >= GRID]
    pending = None
    for iteration in range(ITERS + 1):
        if pending is not None:
            probe_sum = pending
            probe_modes = (
                probe_modes - probe_rate / (slot_count * tile_count * group_count) * probe_sum
            )
        if iteration == ITERS:
            break
        right_part = shifted(obj_state, "tile", -1)
        upper_half = jnp.concatenate([obj_state, right_part], axis=-1)
        lower_half = shifted(upper_half, "tile", -GRID)
        canvas = jnp.concatenate([upper_half, lower_half], axis=-2)
        current_probe = probe_modes

        grad_canvas = jnp.zeros_like(canvas)
        grad_probe = jnp.zeros_like(probe_modes)
        for slot_index in range(slot_count):
            row_start = offsets[0, 0, slot_index, 0]
            col_start = offsets[0, 0, slot_index, 1]
            starts = (anchor, anchor, row_start, col_start)
            patch_cells = lax.dynamic_slice(canvas, starts, (2, slices, pattern_side, pattern_side))
            target = measured[0, 0, slot_index]
            weight = live[0, 0, slot_index].astype(jnp.float32)
            grad_patch, grad_modes = slot_grad(patch_cells, current_probe, target, weight, tables)
            current = lax.dynamic_slice(
                grad_canvas, starts, (2, slices, pattern_side, pattern_side)
            )
            grad_canvas = lax.dynamic_update_slice(grad_canvas, current + grad_patch, starts)
            grad_probe = grad_probe + grad_modes
        if slot_count == 1 and pattern_side == block_side:
            spread = jnp.pad(
                grad_patch, ((0, 0), (0, 0), (block_side, block_side), (block_side, block_side))
            )
            quarter = lambda y0, x0: lax.dynamic_slice(
                spread,
                (anchor, anchor, y0 - row_start, x0 - col_start),
                (2, slices, block_side, block_side),
            )
            grad_ul, grad_ur = (quarter(block_side, block_side), quarter(block_side, 2 * block_side))
            grad_ll = quarter(2 * block_side, block_side)
            grad_lr = quarter(2 * block_side, 2 * block_side)
        else:
            grad_ul = grad_canvas[:, :, :block_side, :block_side]
            grad_ur = grad_canvas[:, :, :block_side, block_side:]
            grad_ll = grad_canvas[:, :, block_side:, :block_side]
            grad_lr = grad_canvas[:, :, block_side:, block_side:]
        planes = lambda a: a.reshape(-1, block_side, block_side)
        probe_partial = a2a_sum(xor_sum(grad_probe, "scan"), "tile")
        sent_down = jnp.concatenate(
            [
                planes(grad_ll),
                planes(grad_lr),
            ]
        )
        came_down = shifted(sent_down, "tile", GRID)
        own_part = planes(grad_ul) + came_down[:parts]
        right_side = planes(grad_ur) + came_down[parts:]
        own_part = own_part + shifted(right_side, "tile", 1)
        grad_total = xor_sum(own_part, "scan").reshape(obj_state.shape)
        pending = probe_partial
        obj_state = obj_state - object_rate / (slot_count * group_count) * grad_total
    return (obj_state[0][:, None], obj_state[1][:, None], probe_modes)


def solution(mesh):
    placed = (
        P(None, "tile", None, None),
        P(None, "tile", None, None),
        P(),
        P("tile", "scan", None, None, None),
        P("tile", "scan", None, None),
        P("tile", "scan", None),
    )
    return jax.shard_map(
        local,
        mesh=mesh,
        in_specs=placed,
        out_specs=(P(None, "tile", None, None), P(None, "tile", None, None), P()),
        check_vma=False,
    )
```

```python
import math

import jax
import jax.numpy as jnp
from jax import lax
from jax.experimental import pallas as pl
from jax.experimental.pallas import tpu as pltpu
from jax.sharding import PartitionSpec as P

GRID = 8
ITERS = 2


object_rate = 0.008
probe_rate = 0.03


def shifted(shard, axis, by):
    size = lax.axis_size(axis)
    return lax.ppermute(shard, axis, [(i, (i + by) % size) for i in range(size)])


def make_tables(pattern_side):
    positions = lax.iota(jnp.int32, pattern_side)
    product = positions[:, None] * positions[None, :] % pattern_side
    angles = 2.0 * math.pi / pattern_side * product.astype(jnp.float32)
    scaling = 1.0 / math.sqrt(pattern_side)
    frequency = jnp.where(
        positions < pattern_side // 2, positions, positions - pattern_side
    ).astype(jnp.float32)
    phases = (
        -4.0
        * math.pi
        * (frequency[:, None] ** 2 + frequency[None, :] ** 2)
        / (pattern_side * pattern_side)
    )
    return (jnp.cos(angles) * scaling, jnp.sin(angles) * scaling, jnp.cos(phases), jnp.sin(phases))


def from_left(matrix, values):
    return jnp.einsum("jk,mkl->mjl", matrix, values, precision=lax.Precision.HIGHEST)


def from_right(values, matrix):
    return jnp.einsum("mjk,kl->mjl", values, matrix, precision=lax.Precision.HIGHEST)


def transform(part_real, part_imag, tables, sign):
    cosine, sine_table = (tables[0], tables[1])
    left_real = from_left(cosine, part_real) + sign * from_left(sine_table, part_imag)
    left_imag = from_left(cosine, part_imag) - sign * from_left(sine_table, part_real)
    out_real = from_right(left_real, cosine) + sign * from_right(left_imag, sine_table)
    out_imag = from_right(left_imag, cosine) - sign * from_right(left_real, sine_table)
    return (out_real, out_imag)


def slot_loss(patch_cells, mode_values, target, weight, tables):
    depth_count = patch_cells.shape[1]
    wave_real, wave_imag = (mode_values[:, 0], mode_values[:, 1])
    for depth_index in range(depth_count):
        cell_real = patch_cells[0, depth_index]
        cell_imag = patch_cells[1, depth_index]
        wave_real, wave_imag = (
            wave_real * cell_real - wave_imag * cell_imag,
            wave_real * cell_imag + wave_imag * cell_real,
        )
        if depth_index < depth_count - 1:
            freq_real, freq_imag = transform(wave_real, wave_imag, tables, 1.0)
            kern_real, kern_imag = (tables[2], tables[3])
            freq_real, freq_imag = (
                freq_real * kern_real - freq_imag * kern_imag,
                freq_real * kern_imag + freq_imag * kern_real,
            )
            wave_real, wave_imag = transform(freq_real, freq_imag, tables, -1.0)
    far_real, far_imag = transform(wave_real, wave_imag, tables, 1.0)
    intensity = jnp.sum(far_real**2 + far_imag**2, axis=0)
    return 0.5 * weight * jnp.sum((intensity - target) ** 2)


def slot_kernel(cells_ref, probe_ref, target_ref, weight_ref, tab_ref, gcells_ref, gprobe_ref):
    side = target_ref.shape[0]
    mode_count = probe_ref.shape[0]
    depth_count = cells_ref.shape[1]
    wide = lambda a: jnp.concatenate([a] * mode_count, axis=1)
    cosine, sine_table = (tab_ref[0], tab_ref[1])
    kern = (wide(tab_ref[2]), wide(tab_ref[3]))

    stack = lambda a: jnp.concatenate(
        [a[:, m * side : (m + 1) * side] for m in range(mode_count)], axis=0
    )
    unstack = lambda a: jnp.concatenate(
        [a[m * side : (m + 1) * side] for m in range(mode_count)], axis=1
    )

    def dot(a, b):
        return jnp.dot(a, b, precision=lax.Precision.HIGHEST, preferred_element_type=jnp.float32)

    def forward(xr, xi):
        lr = dot(cosine, xr) + dot(sine_table, xi)
        li = dot(cosine, xi) - dot(sine_table, xr)
        lr, li = (stack(lr), stack(li))
        return (
            unstack(dot(lr, cosine) + dot(li, sine_table)),
            unstack(dot(li, cosine) - dot(lr, sine_table)),
        )

    def inverse(xr, xi):
        lr = dot(cosine, xr) - dot(sine_table, xi)
        li = dot(cosine, xi) + dot(sine_table, xr)
        lr, li = (stack(lr), stack(li))
        return (
            unstack(dot(lr, cosine) - dot(li, sine_table)),
            unstack(dot(li, cosine) + dot(lr, sine_table)),
        )

    def mul(a, b):
        return (a[0] * b[0] - a[1] * b[1], a[0] * b[1] + a[1] * b[0])

    def mul_conj(a, b):
        return (a[0] * b[0] + a[1] * b[1], a[1] * b[0] - a[0] * b[1])

    def fold(a):
        total = a[:, :side]
        for m in range(1, mode_count):
            total = total + a[:, m * side : (m + 1) * side]
        return total

    propagate = lambda x: inverse(*mul(forward(*x), kern))
    propagate_adjoint = lambda x: inverse(*mul_conj(forward(*x), kern))
    layers = [(wide(cells_ref[0, d]), wide(cells_ref[1, d])) for d in range(depth_count)]
    wave = (
        jnp.concatenate([probe_ref[m, 0] for m in range(mode_count)], axis=1),
        jnp.concatenate([probe_ref[m, 1] for m in range(mode_count)], axis=1),
    )
    inputs = []
    for d in range(depth_count):
        inputs.append(wave)
        wave = mul(wave, layers[d])
        if d < depth_count - 1:
            wave = propagate(wave)
    far = forward(*wave)
    intensity = fold(far[0] * far[0] + far[1] * far[1])
    residual = wide(weight_ref[...] * (intensity - target_ref[...]))
    grad = inverse(2.0 * residual * far[0], 2.0 * residual * far[1])
    for d in reversed(range(depth_count)):
        term = mul_conj(grad, inputs[d])
        gcells_ref[0, d] = fold(term[0])
        gcells_ref[1, d] = fold(term[1])
        grad = mul_conj(grad, layers[d])
        if d > 0:
            grad = propagate_adjoint(grad)
    for m in range(mode_count):
        gprobe_ref[m, 0] = grad[0][:, m * side : (m + 1) * side]
        gprobe_ref[m, 1] = grad[1][:, m * side : (m + 1) * side]


def slot_grad(patch_cells, mode_values, target, weight, tables):
    tab = jnp.stack(tables)
    side = target.shape[-1]
    dots = 2 * mode_values.shape[0] * 10 * 8
    return pl.pallas_call(
        slot_kernel,
        out_shape=(
            jax.ShapeDtypeStruct(patch_cells.shape, jnp.float32),
            jax.ShapeDtypeStruct(mode_values.shape, jnp.float32),
        ),
        in_specs=[pl.BlockSpec(memory_space=pltpu.VMEM)] * 5,
        out_specs=(pl.BlockSpec(memory_space=pltpu.VMEM), pl.BlockSpec(memory_space=pltpu.VMEM)),
        cost_estimate=pl.CostEstimate(
            flops=dots * 2 * side**3, bytes_accessed=4 * side * side * 22, transcendentals=0
        ),
    )(patch_cells, mode_values, target, weight.reshape(1, 1), tab)


def xor_sum(values, axis, steps=None):
    size = lax.axis_size(axis)
    if steps is None:
        steps = [1 << bit for bit in range(size.bit_length() - 1)]
    for step in steps:
        values = values + lax.ppermute(values, axis, [(i, i ^ step) for i in range(size)])
    return values


def a2a_sum(values, axis):
    size = lax.axis_size(axis)
    flat = values.reshape(size, -1)
    part = jnp.sum(lax.all_to_all(flat, axis, 0, 0, tiled=True), axis=0, keepdims=True)
    spread = lax.all_to_all(jnp.broadcast_to(part, flat.shape), axis, 0, 0, tiled=True)
    return spread.reshape(values.shape)


def local(object_real, object_imag, probe_modes, measured, offsets, live):
    slices = object_real.shape[0]
    block_side = object_real.shape[2]
    pattern_side = probe_modes.shape[2]
    slot_count = measured.shape[2]
    tile_count = lax.axis_size("tile")
    group_count = lax.axis_size("scan")
    tables = make_tables(pattern_side)
    anchor = jnp.zeros((), jnp.int32)
    obj_state = jnp.stack([object_real[:, 0], object_imag[:, 0]])
    parts = 2 * slices
    tile_bits = [1 << bit for bit in range(tile_count.bit_length() - 1)]
    first_bits = [b for b in tile_bits if b < GRID]
    second_bits = [b for b in tile_bits if b >= GRID]
    pending = None
    for iteration in range(ITERS + 1):
        if pending is not None:
            probe_sum = pending
            probe_modes = (
                probe_modes - probe_rate / (slot_count * tile_count * group_count) * probe_sum
            )
        if iteration == ITERS:
            break
        right_part = shifted(obj_state, "tile", -1)
        upper_half = jnp.concatenate([obj_state, right_part], axis=-1)
        lower_half = shifted(upper_half, "tile", -GRID)
        canvas = jnp.concatenate([upper_half, lower_half], axis=-2)
        current_probe = probe_modes

        grad_canvas = jnp.zeros_like(canvas)
        grad_probe = jnp.zeros_like(probe_modes)
        for slot_index in range(slot_count):
            row_start = offsets[0, 0, slot_index, 0]
            col_start = offsets[0, 0, slot_index, 1]
            starts = (anchor, anchor, row_start, col_start)
            patch_cells = lax.dynamic_slice(canvas, starts, (2, slices, pattern_side, pattern_side))
            target = measured[0, 0, slot_index]
            weight = live[0, 0, slot_index].astype(jnp.float32)
            grad_patch, grad_modes = slot_grad(patch_cells, current_probe, target, weight, tables)
            current = lax.dynamic_slice(
                grad_canvas, starts, (2, slices, pattern_side, pattern_side)
            )
            grad_canvas = lax.dynamic_update_slice(grad_canvas, current + grad_patch, starts)
            grad_probe = grad_probe + grad_modes
        if slot_count == 1 and pattern_side == block_side:
            spread = jnp.pad(
                grad_patch, ((0, 0), (0, 0), (block_side, block_side), (block_side, block_side))
            )
            quarter = lambda y0, x0: lax.dynamic_slice(
                spread,
                (anchor, anchor, y0 - row_start, x0 - col_start),
                (2, slices, block_side, block_side),
            )
            grad_ul, grad_ur = (quarter(block_side, block_side), quarter(block_side, 2 * block_side))
            grad_ll = quarter(2 * block_side, block_side)
            grad_lr = quarter(2 * block_side, 2 * block_side)
        else:
            grad_ul = grad_canvas[:, :, :block_side, :block_side]
            grad_ur = grad_canvas[:, :, :block_side, block_side:]
            grad_ll = grad_canvas[:, :, block_side:, :block_side]
            grad_lr = grad_canvas[:, :, block_side:, block_side:]
        planes = lambda a: a.reshape(-1, block_side, block_side)
        sent_down = jnp.concatenate(
            [
                planes(grad_ll),
                planes(grad_lr),
            ]
        )
        pair = lambda a, b: lax.optimization_barrier((a, b))
        probe_partial = xor_sum(grad_probe, "scan", [1])
        sent_down, probe_partial = pair(sent_down, probe_partial)
        came_down = shifted(sent_down, "tile", GRID)
        probe_partial = xor_sum(probe_partial, "scan", [2])
        own_part = planes(grad_ul) + came_down[:parts]
        right_side = planes(grad_ur) + came_down[parts:]
        right_side, probe_partial = pair(right_side, probe_partial)
        came_left = shifted(right_side, "tile", 1)
        probe_partial = xor_sum(probe_partial, "scan", [4])
        own_part = own_part + came_left
        own_part, probe_partial = pair(own_part, probe_partial)
        probe_partial = a2a_sum(probe_partial, "tile")
        grad_total = xor_sum(own_part, "scan").reshape(obj_state.shape)
        pending = probe_partial
        obj_state = obj_state - object_rate / (slot_count * group_count) * grad_total
    return (obj_state[0][:, None], obj_state[1][:, None], probe_modes)


def solution(mesh):
    placed = (
        P(None, "tile", None, None),
        P(None, "tile", None, None),
        P(),
        P("tile", "scan", None, None, None),
        P("tile", "scan", None, None),
        P("tile", "scan", None),
    )
    return jax.shard_map(
        local,
        mesh=mesh,
        in_specs=placed,
        out_specs=(P(None, "tile", None, None), P(None, "tile", None, None), P()),
        check_vma=False,
    )
```
